32 devices in a mesh: tm: 8 (over z, core), space: 4 (over y, x).
Axes of the slice: x: 2, y: 2, z: 4, core: 2. Of those that a mesh axis runs over, the one named last changes fastest.
Arguments:
- initial_temp: float32 [64, 32, 256], P('space'), may hold values from -6 to 6
- region_labels: int32 [16, 8, 64], P('space'), may hold values from 0 to 5
- region_rate: float32 [6], replicated, may hold values from 0.5 to 8
- heat_rate: float32 [8, 6], replicated, may hold values from 0.1 to 2
Outputs:
- slice_end: float32 [8, 64, 32, 256], P('tm', 'space')
The draws below stay inside these ranges and needn't reach their ends.
All inputs are finite; a program needn't handle non-finite values.
Results may differ from the reference program's by a relative error of at most 0.0001.
Values sent between devices are 32-bit elements; how exact they have to be, the bound alone decides.
A program may use at most 128 MiB of HBM per device.

```python
import math
import jax
import jax.numpy as jnp
from jax import lax

NY = 32
NZ = 256
FINE_STEPS = 2
SWEEPS = 8
C_SWEEPS = 4
PARA_ITERS = 2
REGIONS = 6
SLICES = 8
NX = 64


def with_ends(drawn, key, least, top_value):
    longest = drawn.shape.index(max(drawn.shape))
    spots = []
    for shift in (0, 1):
        where = [jax.random.randint(jax.random.fold_in(key, axis), (), 0, length) for axis, length in enumerate(drawn.shape)]
        where[longest] = (where[longest] + shift) % drawn.shape[longest]
        spots.append(tuple(where))
    return drawn.at[spots[0]].set(least).at[spots[1]].set(top_value)


def level_of(stream_key, extent, cuts, smallest, top_value):
    factor_of = 1.0
    for axis_at, shards_of in cuts:
        steps = jax.random.uniform(jax.random.fold_in(jax.random.fold_in(stream_key, 6), axis_at), (shards_of,), jnp.float32, smallest / len(cuts), top_value / len(cuts))
        factor_of = factor_of * jnp.repeat(jnp.exp(steps), extent[axis_at] // shards_of).reshape((-1,) + (1,) * (len(extent) - 1 - axis_at))
    return factor_of


def scatter_about(stream_key, shape, width, reach, shards=(), held_as=jnp.bfloat16):
    gain = level_of(stream_key, shape, shards, -0.22, 0.18) if shards else 1.0
    drawn = jax.random.normal(stream_key, shape, jnp.float32) * width * gain
    return jnp.minimum(jnp.maximum(drawn, -reach), reach).astype(held_as)


def setup_inputs(seed: int = 0) -> dict:
    seeds = jax.random.split(jax.random.key(seed), 5)
    return {
        "initial_temp": scatter_about(seeds[0], (NX, NY, NZ), 1.0, 6.0, ((0, 4),), jnp.float32),
        "region_labels": with_ends(jax.random.randint(seeds[1], (NX // 4, NY // 4, NZ // 4), 0, REGIONS), jax.random.fold_in(seeds[1], 1), 0, REGIONS - 1).astype(jnp.int32),
        "region_rate": jnp.clip(jnp.exp(jax.random.uniform(seeds[2], (REGIONS,), jnp.float32, math.log(0.5), math.log(8.0))), 0.5, 8.0),
        "heat_rate": jnp.clip(jax.random.uniform(seeds[3], (SLICES, REGIONS), jnp.float32, 0.1, 2.0), 0.1, 2.0),
    }


def neighbours(field):
    padded = jnp.pad(field, 1)
    total = padded[2:, 1:-1, 1:-1] + padded[:-2, 1:-1, 1:-1]
    total = total + padded[1:-1, 2:, 1:-1] + padded[1:-1, :-2, 1:-1]
    total = total + padded[1:-1, 1:-1, 2:] + padded[1:-1, 1:-1, :-2]
    return total


def expand(block):
    lead = block.shape[:-3]
    sx, sy, sz = block.shape[-3:]
    wide = jnp.broadcast_to(block[..., :, None, :, None, :, None], lead + (sx, 4, sy, 4, sz, 4))
    return wide.reshape(lead + (4 * sx, 4 * sy, 4 * sz))


def restrict(field):
    lead = field.shape[:-3]
    sx, sy, sz = field.shape[-3:]
    split = field.reshape(lead + (sx // 4, 4, sy // 4, 4, sz // 4, 4))
    return jnp.mean(split, axis=(-5, -3, -1))


def propagate(state, inverse, weight, source, count, sweeps):
    for outer_index in range(count):
        scaled = (state + source) * inverse
        field = state
        for sweep_index in range(sweeps):
            field = scaled + weight * neighbours(field)
        state = field
    return state


def reference(initial_temp, region_labels, region_rate, heat_rate):
    rate = region_rate[region_labels]
    rate_fine = expand(rate)
    inv_fine = 1.0 / (1.0 + 6.0 * rate_fine)
    weight_fine = rate_fine * inv_fine
    rate_coarse = FINE_STEPS * rate / 16.0
    inv_coarse = 1.0 / (1.0 + 6.0 * rate_coarse)
    weight_coarse = rate_coarse * inv_coarse

    def fine_one(state, row):
        return propagate(state, inv_fine, weight_fine, expand(row[region_labels]), FINE_STEPS, SWEEPS)

    def coarse_one(coarse, row):
        return propagate(coarse, inv_coarse, weight_coarse, FINE_STEPS * row[region_labels], 1, C_SWEEPS)

    start = restrict(initial_temp)

    def chain(deltas):
        def advance(coarse, pair):
            row, delta = pair
            return coarse_one(coarse, row) + delta, coarse

        unused, starts = lax.scan(advance, start, (heat_rate, deltas))
        return starts, jax.vmap(coarse_one)(starts, heat_rate)

    starts, ends = chain(jnp.zeros((SLICES,) + start.shape, jnp.float32))
    states = jnp.concatenate([initial_temp[None], expand(starts[1:])], axis=0)
    corrected = states
    for iteration in range(PARA_ITERS):
        fine_ends = jax.vmap(fine_one)(states, heat_rate)
        starts, new_ends = chain(restrict(fine_ends) - ends)
        corrected = fine_ends + expand(new_ends - ends)
        ends = new_ends
        states = jnp.concatenate([initial_temp[None], corrected[:-1]], axis=0)
    return corrected
```

```python
import functools

import jax
import jax.numpy as jnp
from jax import lax
from jax.experimental import pallas as pl
from jax.experimental.pallas import tpu as pltpu
from jax.sharding import PartitionSpec as P

FINE_STEPS = 2
SWEEPS = 8
C_SWEEPS = 4
W1 = FINE_STEPS * SWEEPS
W2 = SWEEPS
F32 = jnp.float32
MESH = pl.DeviceIdType.MESH
HI = lax.Precision.HIGHEST


def dot(a, b):
    return jnp.dot(a, b, precision=HI, preferred_element_type=F32)


def select_matrix(shape, small_axis):
    small = lax.broadcasted_iota(jnp.int32, shape, small_axis)
    large = lax.broadcasted_iota(jnp.int32, shape, 1 - small_axis)
    hit = (large >= 4 * small) & (large < 4 * small + 4)
    return jnp.where(hit, F32(1.0), F32(0.0))


def kernel(
    n_count, s_count,
    init, labels, rates, heat,
    out,
    ag, gag, t0, u, sc, wt, inv, src, fs, fr, mid, kp, es, er, cs, cr, dcur,
    ag_ss, ag_rs, ih_ss, ih_rs, f_ss, f_rs, m_ss, m_rs, e_ss, e_rs, c_ss, c_rs,
):
    n = lax.axis_index("tm")
    s = lax.axis_index("space")
    planes, ny, nz = init.shape
    bx, cy, cz = labels.shape
    cx = bx * s_count
    lanes = ag.shape[-1]
    regions = rates.shape[1]
    pad = W1 // 4
    has_prev, has_next = n > 0, n < n_count - 1
    has_lo, has_hi = s > 0, s < s_count - 1

    barrier = pltpu.get_barrier_semaphore()
    def greet(cond, dev):
        @pl.when(cond)
        def _():
            pl.semaphore_signal(barrier, inc=1, device_id=dev, device_id_type=MESH)
    def one(c):
        return jnp.where(c, 1, 0).astype(jnp.int32)
    for j in range(1, s_count):
        pl.semaphore_signal(
            barrier, inc=1, device_id=(n, lax.rem(s + j, s_count)), device_id_type=MESH)
    partners = s_count - 1
    for cond_n, dn in ((has_prev, -1), (has_next, 1)):
        for cond_s, ds in ((None, 0), (has_lo, -1), (has_hi, 1)):
            cond = cond_n if cond_s is None else cond_n & cond_s
            greet(cond, (n + dn, s + ds))
            partners = partners + one(cond)
    pl.semaphore_wait(barrier, partners)

    def remote(a, b, ss, rs, dev):
        return pltpu.make_async_remote_copy(
            src_ref=a, dst_ref=b, send_sem=ss, recv_sem=rs, device_id=dev, device_id_type=MESH)

    ez = select_matrix((lanes, nz), 0)
    ey = select_matrix((ny, cy), 1)
    rz = select_matrix((nz, lanes), 1)
    ry = select_matrix((cy, ny), 0)

    def expand(block):
        return dot(ey, dot(block, ez))

    def restrict_plane(total):
        return dot(dot(ry, total), rz) * F32(1.0 / 64.0)

    def lookup(lab, row):
        total = jnp.zeros(lab.shape, F32)
        for r in range(regions):
            total = total + jnp.where(lab == F32(r), row(r), F32(0.0))
        return total

    crow = lax.broadcasted_iota(jnp.int32, (cx, cy, lanes), 1)
    c_first, c_last = crow == 0, crow == cy - 1
    czero = jnp.zeros((1, cy, lanes), F32)

    def c_neighbours(w):
        total = jnp.concatenate([czero, w[:-1]], 0) + jnp.concatenate([w[1:], czero], 0)
        total = total + jnp.where(c_first, F32(0.0), pltpu.roll(w, 1, 1))
        total = total + jnp.where(c_last, F32(0.0), pltpu.roll(w, cy - 1, 1))
        return total + (pltpu.roll(w, 1, 2) + pltpu.roll(w, lanes - 1, 2))

    def c_jacobi(scaled, w, c_weight):
        for _ in range(C_SWEEPS):
            w = scaled + c_weight * c_neighbours(w)
        return w

    frow = lax.broadcasted_iota(jnp.int32, (ny, nz), 0)
    fcol = lax.broadcasted_iota(jnp.int32, (ny, nz), 1)
    y_first, y_last = frow == 0, frow == ny - 1
    z_first, z_last = fcol == 0, fcol == nz - 1

    def in_plane(w):
        a = jnp.where(y_first, F32(0.0), pltpu.roll(w, 1, 0))
        b = jnp.where(y_last, F32(0.0), pltpu.roll(w, ny - 1, 0))
        c = jnp.where(z_first, F32(0.0), pltpu.roll(w, 1, 1))
        d = jnp.where(z_last, F32(0.0), pltpu.roll(w, nz - 1, 1))
        return (a + b) + (c + d)

    def fine_step(first, length, shrink):
        def scale(q, _):
            p = first + q
            sc[p] = (u[p + 1] + src[p]) * inv[p]
            return 0
        lax.fori_loop(0, length, scale, 0)

        def sweep(i, _):
            cut = 2 * (i // 2)
            lo = first + cut

            def quad(q, carry):
                before, cur = carry
                for r in range(4):
                    p = lo + 4 * q + r
                    after = u[p + 2]
                    u[p + 1] = sc[p] + wt[p] * ((before + after) + in_plane(cur))
                    before, cur = cur, after
                return before, cur

            lax.fori_loop(0, (length - 2 * cut) // 4, quad, (u[lo], u[lo + 1]))
            return 0
        lax.fori_loop(0, shrink, sweep, 0)

    def gather_start(stage, ref, mine):
        copies = []
        for j in range(1, s_count):
            copy = remote(mine(ref), mine(ref), ag_ss.at[stage, j], ag_rs.at[stage, j],
                          (n, lax.rem(s + j, s_count)))
            copy.start()
            copies.append(copy)
        return copies

    own = pl.ds(pad + bx * s, bx)

    ext = W1 * 2 + planes
    zero_block = jnp.zeros((pad, cy, lanes), F32)
    for k in (0, pad + cx):
        ag[0, k:k + pad] = zero_block
        ag[1, k:k + pad] = zero_block - 1.0
        kp[k:k + pad] = zero_block
    zero_fine = jnp.zeros((ny, nz), F32)
    u[0] = zero_fine
    u[ext + 1] = zero_fine

    def restricted(plane_of, ref, lead):
        for k in range(bx):
            total = (plane_of(4 * k) + plane_of(4 * k + 1)) + (plane_of(4 * k + 2) + plane_of(4 * k + 3))
            value = restrict_plane(total)
            if lead:
                ref[0, pad + bx * s + k] = value
            else:
                ref[bx * s + k] = value

    restricted(lambda p: init[p], ag, True)
    lane_pad = jnp.full((bx, cy, lanes - cz), -1.0, F32)
    ag[1, own] = jnp.concatenate([labels[...].astype(F32), lane_pad], axis=2)
    g0 = gather_start(0, ag, lambda r: r.at[:, own])

    first_slice = n == 0
    ih_lo = remote(init, t0.at[pl.ds(W1 + planes, W1)], ih_ss.at[0], ih_rs.at[0], (n, s - 1))
    ih_hi = remote(init, t0.at[pl.ds(0, W1)], ih_ss.at[1], ih_rs.at[1], (n, s + 1))

    @pl.when(first_slice & has_lo)
    def _():
        ih_lo.start()

    @pl.when(first_slice & has_hi)
    def _():
        ih_hi.start()

    @pl.when(jnp.logical_not(has_lo))
    def _():
        t0[0:W1] = jnp.zeros((W1, ny, nz), F32)
        fr[0:W2] = jnp.zeros((W2, ny, nz), F32)
        mid[0] = jnp.zeros((W2, ny, nz), F32)

    @pl.when(jnp.logical_not(has_hi))
    def _():
        t0[W1 + planes:] = jnp.zeros((W1, ny, nz), F32)
        fr[W2 + planes:] = jnp.zeros((W2, ny, nz), F32)
        mid[1] = jnp.zeros((W2, ny, nz), F32)

    for copy in g0:
        copy.wait()

    def coeff(k, _):
        lab = ag[1, bx * s + k]
        rate = lookup(lab, lambda r: rates[0, r])
        iv = 1.0 / (1.0 + 6.0 * rate)
        we = rate * iv
        so = lookup(lab, lambda r: heat[n, r])
        fi, fw, fo = expand(iv), expand(we), expand(so)
        for r in range(4):
            inv[4 * k + r] = fi
            wt[4 * k + r] = fw
            src[4 * k + r] = fo
        return 0
    lax.fori_loop(0, ext // 4, coeff, 0)

    lab_all = ag[1, pad:pad + cx]
    c_rate = FINE_STEPS * lookup(lab_all, lambda r: rates[0, r]) / 16.0
    c_inv = 1.0 / (1.0 + 6.0 * c_rate)
    c_weight = c_rate * c_inv

    def advance(m, c):
        source = FINE_STEPS * lookup(lab_all, lambda r: heat[m, r])
        return c_jacobi((c + source) * c_inv, c, c_weight)

    own_c = lax.fori_loop(0, n, advance, ag[0, pad:pad + cx])
    dcur[...] = advance(n, own_c)
    kp[pad:pad + cx] = own_c

    @pl.when(first_slice)
    def _():
        @pl.when(has_hi)
        def _():
            ih_lo_wait = remote(init, t0.at[pl.ds(W1 + planes, W1)], ih_ss.at[0], ih_rs.at[0], (n, s + 1))
            ih_lo_wait.wait_recv()

        @pl.when(has_lo)
        def _():
            ih_hi_wait = remote(init, t0.at[pl.ds(0, W1)], ih_ss.at[1], ih_rs.at[1], (n, s - 1))
            ih_hi_wait.wait_recv()

        def lay(p, _):
            u[1 + p] = t0[p]
            u[1 + W1 + planes + p] = t0[W1 + planes + p]
            return 0
        lax.fori_loop(0, W1, lay, 0)

        def lay_own(p, _):
            u[1 + W1 + p] = init[p]
            return 0
        lax.fori_loop(0, planes, lay_own, 0)

    @pl.when(has_prev)
    def _():
        def lay(k, _):
            f = expand(kp[bx * s + k])
            for r in range(4):
                u[1 + 4 * k + r] = f
            return 0
        lax.fori_loop(0, ext // 4, lay, 0)

    fine_step(0, ext, SWEEPS)
    fine_step(SWEEPS, ext - 2 * SWEEPS, SWEEPS)

    own_g = pl.ds(bx * s, bx)

    def coarse_part(stage, plane_of):
        restricted(plane_of, gag.at[stage], False)
        copies = gather_start(stage + 1, gag.at[stage], lambda r: r.at[own_g])
        return copies

    def keep(p, _):
        fs[p] = u[1 + W1 + p]
        return 0
    lax.fori_loop(0, planes, keep, 0)
    g1 = coarse_part(0, lambda p: fs[p])

    f_own = remote(fs, fr.at[pl.ds(W2, planes)], f_ss.at[0], f_rs.at[0], (n + 1, s))
    f_lo = remote(fs.at[pl.ds(0, W2)], fr.at[pl.ds(W2 + planes, W2)], f_ss.at[1], f_rs.at[1], (n + 1, s - 1))
    f_hi = remote(fs.at[pl.ds(planes - W2, W2)], fr.at[pl.ds(0, W2)], f_ss.at[2], f_rs.at[2], (n + 1, s + 1))

    @pl.when(has_next)
    def _():
        f_own.start()

    @pl.when(has_next & has_lo)
    def _():
        f_lo.start()

    @pl.when(has_next & has_hi)
    def _():
        f_hi.start()

    for copy in g1:
        copy.wait()

    def chain(stage):
        e_copy = remote(es.at[stage], er.at[stage], e_ss.at[stage], e_rs.at[stage], (n + 1, s))

        @pl.when(first_slice)
        def _():
            er[stage] = jnp.zeros((cx, cy, lanes), F32)

        @pl.when(has_prev)
        def _():
            e_copy.wait_recv()
        e = er[stage]
        corr = c_jacobi(e * c_inv, e, c_weight)
        rf = gag[stage]
        es[stage] = corr + (rf - dcur[...])

        @pl.when(has_next)
        def _():
            e_copy.start()
        dcur[...] = rf + corr
        return corr

    cs[...] = chain(0)
    c_copy = remote(cs, cr, c_ss, c_rs, (n + 1, s))

    @pl.when(has_next)
    def _():
        c_copy.start()

    off = W1 - W2
    span = planes + 2 * W2

    @pl.when(first_slice)
    def _():
        def lay(p, _):
            u[1 + off + p] = t0[off + p]
            u[1 + W1 + planes + p] = t0[W1 + planes + p]
            return 0
        lax.fori_loop(0, W2, lay, 0)

        def lay_own(p, _):
            u[1 + W1 + p] = init[p]
            return 0
        lax.fori_loop(0, planes, lay_own, 0)

    @pl.when(has_prev)
    def _():
        c_copy.wait_recv()
        f_own.wait_recv()

        @pl.when(has_hi)
        def _():
            f_lo.wait_recv()

        @pl.when(has_lo)
        def _():
            f_hi.wait_recv()
        kp[pad:pad + cx] = cr[...]

        def lay(k, _):
            f = expand(kp[bx * s + off // 4 + k])
            for r in range(4):
                u[1 + off + 4 * k + r] = fr[4 * k + r] + f
            return 0
        lax.fori_loop(0, span // 4, lay, 0)

    fine_step(off, span, SWEEPS)

    m_lo = remote(u.at[pl.ds(1 + W1, W2)], mid.at[1], m_ss.at[0], m_rs.at[0], (n, s - 1))
    m_hi = remote(u.at[pl.ds(1 + W1 + planes - W2, W2)], mid.at[0], m_ss.at[1], m_rs.at[1], (n, s + 1))

    @pl.when(has_lo)
    def _():
        m_lo.start()

    @pl.when(has_hi)
    def _():
        m_hi.start()

    @pl.when(has_lo)
    def _():
        m_hi.wait_recv()
        m_lo.wait_send()

    @pl.when(has_hi)
    def _():
        m_lo.wait_recv()
        m_hi.wait_send()

    def lay_mid(p, _):
        u[1 + off + p] = mid[0, p]
        u[1 + W1 + planes + p] = mid[1, p]
        return 0
    lax.fori_loop(0, W2, lay_mid, 0)
    fine_step(off, span, SWEEPS)

    g2 = coarse_part(1, lambda p: u[1 + W1 + p])
    for copy in g2:
        copy.wait()
    kp[pad:pad + cx] = chain(1)

    def finish(k, _):
        f = expand(kp[pad + bx * s + k])
        for r in range(4):
            out[0, 4 * k + r] = u[1 + W1 + 4 * k + r] + f
        return 0
    lax.fori_loop(0, bx, finish, 0)

    @pl.when(first_slice & has_lo)
    def _():
        ih_lo.wait_send()

    @pl.when(first_slice & has_hi)
    def _():
        ih_hi.wait_send()

    @pl.when(has_next)
    def _():
        f_own.wait_send()
        c_copy.wait_send()
        for stage in range(2):
            remote(es.at[stage], er.at[stage], e_ss.at[stage], e_rs.at[stage], (n + 1, s)).wait_send()

    @pl.when(has_next & has_lo)
    def _():
        f_lo.wait_send()

    @pl.when(has_next & has_hi)
    def _():
        f_hi.wait_send()


def solution(mesh):
    n_count, s_count = mesh.shape["tm"], mesh.shape["space"]

    def on_device(init, labels, rates, heat):
        planes, ny, nz = init.shape
        bx, cy, cz = labels.shape
        cx = bx * s_count
        lanes = 128 * (cz // 128 + 1)
        pad = W1 // 4
        ext = planes + 2 * W1
        dma = pltpu.SemaphoreType.DMA

        def vm(*shape):
            return pltpu.VMEM(shape, F32)

        vmem = pl.BlockSpec(memory_space=pltpu.VMEM)
        smem = pl.BlockSpec(memory_space=pltpu.SMEM)
        return pl.pallas_call(
            functools.partial(kernel, n_count, s_count),
            out_shape=jax.ShapeDtypeStruct((1, planes, ny, nz), F32),
            in_specs=[vmem, vmem, smem, smem],
            out_specs=vmem,
            scratch_shapes=[
                vm(2, cx + 2 * pad, cy, lanes),
                vm(2, cx, cy, lanes),
                vm(ext, ny, nz),
                vm(ext + 2, ny, nz),
                vm(ext, ny, nz), vm(ext, ny, nz), vm(ext, ny, nz), vm(ext, ny, nz),
                vm(planes, ny, nz),
                vm(planes + 2 * W2, ny, nz),
                vm(2, W2, ny, nz),
                vm(cx + 2 * pad, cy, lanes),
                vm(2, cx, cy, lanes), vm(2, cx, cy, lanes),
                vm(cx, cy, lanes), vm(cx, cy, lanes), vm(cx, cy, lanes),
                dma((3, s_count)), dma((3, s_count)),
                dma((2,)), dma((2,)),
                dma((3,)), dma((3,)),
                dma((2,)), dma((2,)),
                dma((2,)), dma((2,)),
                dma(()), dma(()),
            ],
            compiler_params=pltpu.CompilerParams(
                collective_id=0, has_side_effects=True, vmem_limit_bytes=48 * 1024 * 1024),
            name="parareal",
        )(init, labels, rates.reshape(1, -1), heat)

    return jax.shard_map(
        on_device,
        mesh=mesh,
        in_specs=(P("space", None, None), P("space", None, None), P(), P()),
        out_specs=P("tm", "space", None, None),
        check_vma=False,
    )
```

```python
import functools

import jax
import jax.numpy as jnp
from jax import lax
from jax.experimental import pallas as pl
from jax.experimental.pallas import tpu as pltpu
from jax.sharding import PartitionSpec as P

FINE_STEPS = 2
SWEEPS = 8
C_SWEEPS = 4
W1 = FINE_STEPS * SWEEPS
W2 = SWEEPS
F32 = jnp.float32
MESH = pl.DeviceIdType.MESH
HI = lax.Precision.HIGHEST


def dot(a, b):
    return jnp.dot(a, b, precision=HI, preferred_element_type=F32)


def kernel(
    n_count, s_count,
    init_hbm, labels_hbm, rates_hbm, heat_hbm,
    out,
    raw, labels, rates, heat, in_sem, init,
    ag, gag, t0, u, sc, wt, inv, src, fs, fr, mid, kp, es, er, cs, cr, dcur,
    ag_ss, ag_rs, ih_ss, ih_rs, f_ss, f_rs, m_ss, m_rs, e_ss, e_rs, c_ss, c_rs,
):
    n = lax.axis_index("tm")
    s = lax.axis_index("space")
    planes, ny, nz = init_hbm.shape
    bx, cy, cz = labels_hbm.shape
    cx = bx * s_count
    lanes = ag.shape[-1]
    ts, zs = ny // cy, nz // lanes
    regions = rates_hbm.shape[1]
    pad = W1 // 4
    has_prev, has_next = n > 0, n < n_count - 1
    has_lo, has_hi = s > 0, s < s_count - 1

    fetches = [pltpu.make_async_copy(a, b, in_sem.at[i]) for i, (a, b) in enumerate(
        ((init_hbm, raw), (labels_hbm, labels), (rates_hbm, rates), (heat_hbm, heat)))]
    for fetch in fetches:
        fetch.start()

    barrier = pltpu.get_barrier_semaphore()
    def greet(cond, dev):
        @pl.when(cond)
        def _():
            pl.semaphore_signal(barrier, inc=1, device_id=dev, device_id_type=MESH)
    def one(c):
        return jnp.where(c, 1, 0).astype(jnp.int32)
    for j in range(1, s_count):
        pl.semaphore_signal(
            barrier, inc=1, device_id=(n, lax.rem(s + j, s_count)), device_id_type=MESH)
    partners = s_count - 1
    for cond_n, dn in ((has_prev, -1), (has_next, 1)):
        for cond_s, ds in ((None, 0), (has_lo, -1), (has_hi, 1)):
            cond = cond_n if cond_s is None else cond_n & cond_s
            greet(cond, (n + dn, s + ds))
            partners = partners + one(cond)
    pl.semaphore_wait(barrier, partners)

    def remote(a, b, ss, rs, dev):
        return pltpu.make_async_remote_copy(
            src_ref=a, dst_ref=b, send_sem=ss, recv_sem=rs, device_id=dev, device_id_type=MESH)

    half = 4 // zs

    def restrict(planes4):
        total = planes4[0]
        for extra in planes4[1:]:
            total = total + extra
        part = total[0]
        for k in range(1, ts * zs):
            part = part + total[k]
        lane = lax.broadcasted_iota(jnp.int32, part.shape, 1)
        step = 1
        while step < half:
            swap = jnp.where(lane % (2 * step) < step,
                             pltpu.roll(part, lanes - step, 1), pltpu.roll(part, step, 1))
            part = part + swap
            step *= 2
        return part * F32(1.0 / 64.0)

    def lookup(lab, row):
        total = jnp.zeros(lab.shape, F32)
        for r in range(regions):
            total = total + jnp.where(lab == F32(r), row(r), F32(0.0))
        return total

    crow = lax.broadcasted_iota(jnp.int32, (cx, cy, lanes), 1)
    ccol = lax.broadcasted_iota(jnp.int32, (cx, cy, lanes), 2)
    c_first, c_last = crow == 0, crow == cy - 1
    cz_first, cz_last = ccol < half, ccol >= lanes - half
    czero = jnp.zeros((1, cy, lanes), F32)

    def c_neighbours(w):
        total = jnp.concatenate([czero, w[:-1]], 0) + jnp.concatenate([w[1:], czero], 0)
        total = total + (jnp.where(c_first, F32(0.0), pltpu.roll(w, 1, 1))
                         + jnp.where(c_last, F32(0.0), pltpu.roll(w, cy - 1, 1)))
        return total + (jnp.where(cz_first, F32(0.0), pltpu.roll(w, half, 2))
                        + jnp.where(cz_last, F32(0.0), pltpu.roll(w, lanes - half, 2)))

    def c_jacobi(scaled, w, c_weight):
        for _ in range(C_SWEEPS):
            w = scaled + c_weight * c_neighbours(w)
        return w

    row = lax.broadcasted_iota(jnp.int32, (cy, lanes), 0)
    col = lax.broadcasted_iota(jnp.int32, (cy, lanes), 1)
    y_first, y_last = row == 0, row == cy - 1
    z_first, z_last = col == 0, col == lanes - 1

    def in_plane(w, k):
        t, c = k // zs, k % zs
        if t > 0:
            a = w[k - zs]
        else:
            a = jnp.where(y_first, F32(0.0), pltpu.roll(w[(ts - 1) * zs + c], 1, 0))
        if t < ts - 1:
            b = w[k + zs]
        else:
            b = jnp.where(y_last, F32(0.0), pltpu.roll(w[c], cy - 1, 0))
        if c > 0:
            d = w[k - 1]
        else:
            d = jnp.where(z_first, F32(0.0), pltpu.roll(w[k + zs - 1], 1, 1))
        if c < zs - 1:
            e = w[k + 1]
        else:
            e = jnp.where(z_last, F32(0.0), pltpu.roll(w[k - zs + 1], lanes - 1, 1))
        return (a + b) + (d + e)

    tiles = ts * zs

    def fine_step(first, length, shrink):
        def scale(q, _):
            g = first // 4 + q
            iv, so = inv[g], src[g]
            for r in range(4):
                p = first + 4 * q + r
                for k in range(tiles):
                    sc[p, k] = (u[p + 1, k] + so) * iv
            return 0
        lax.fori_loop(0, length // 4, scale, 0)

        def sweep(i, _):
            cut = 4 * (i // 4)
            lo = first + cut

            def quad(q, carry):
                before, cur = carry
                we = wt[lo // 4 + q]
                for r in range(4):
                    p = lo + 4 * q + r
                    after = [u[p + 2, k] for k in range(tiles)]
                    for k in range(tiles):
                        u[p + 1, k] = sc[p, k] + we * ((before[k] + after[k]) + in_plane(cur, k))
                    before, cur = cur, after
                return before, cur

            lax.fori_loop(0, (length - 2 * cut) // 4, quad,
                          ([u[lo, k] for k in range(tiles)], [u[lo + 1, k] for k in range(tiles)]))
            return 0
        lax.fori_loop(0, shrink, sweep, 0)

    def gather_start(stage, ref, mine):
        copies = []
        for j in range(1, s_count):
            copy = remote(mine(ref), mine(ref), ag_ss.at[stage, j], ag_rs.at[stage, j],
                          (n, lax.rem(s + j, s_count)))
            copy.start()
            copies.append(copy)
        return copies

    own = pl.ds(pad + bx * s, bx)

    ext = W1 * 2 + planes
    zero_block = jnp.zeros((pad, cy, lanes), F32)
    for k in (0, pad + cx):
        ag[0, k:k + pad] = zero_block
        ag[1, k:k + pad] = zero_block - 1.0
        kp[k:k + pad] = zero_block
    def zeros(*lead):
        return jnp.zeros(lead + (tiles, cy, lanes), F32)

    zero_fine = zeros()
    u[0] = zero_fine
    u[ext + 1] = zero_fine

    for fetch in fetches:
        fetch.wait()

    zi = lax.broadcasted_iota(jnp.int32, (nz, nz), 0)
    zj = lax.broadcasted_iota(jnp.int32, (nz, nz), 1)
    to_tiles = jnp.where(zi == zs * (zj % lanes) + zj // lanes, F32(1.0), F32(0.0))

    yi = lax.broadcasted_iota(jnp.int32, (ny, ny), 0)
    yj = lax.broadcasted_iota(jnp.int32, (ny, ny), 1)
    rows_to_tiles = jnp.where(yj == ts * (yi % cy) + yi // cy, F32(1.0), F32(0.0))

    def load(p, _):
        moved = dot(rows_to_tiles, dot(raw[p], to_tiles))
        for t in range(ts):
            for c in range(zs):
                init[p, t * zs + c] = moved[t * cy:(t + 1) * cy, c * lanes:(c + 1) * lanes]
        return 0
    lax.fori_loop(0, planes, load, 0, unroll=2)

    li = lax.broadcasted_iota(jnp.int32, (cz, lanes), 0)
    lj = lax.broadcasted_iota(jnp.int32, (cz, lanes), 1)
    spread = jnp.where(li == lj // half, F32(1.0), F32(0.0))
    for k in range(bx):
        ag[0, pad + bx * s + k] = restrict([init[4 * k + r] for r in range(4)])
        ag[1, pad + bx * s + k] = dot(labels[k].astype(F32), spread)
    g0 = gather_start(0, ag, lambda r: r.at[:, own])

    first_slice = n == 0
    ih_lo = remote(init, t0.at[pl.ds(W1 + planes, W1)], ih_ss.at[0], ih_rs.at[0], (n, s - 1))
    ih_hi = remote(init, t0.at[pl.ds(0, W1)], ih_ss.at[1], ih_rs.at[1], (n, s + 1))

    @pl.when(first_slice & has_lo)
    def _():
        ih_lo.start()

    @pl.when(first_slice & has_hi)
    def _():
        ih_hi.start()

    @pl.when(jnp.logical_not(has_lo))
    def _():
        t0[0:W1] = zeros(W1)
        fr[0:W2] = zeros(W2)
        mid[0] = zeros(W2)

    @pl.when(jnp.logical_not(has_hi))
    def _():
        t0[W1 + planes:] = zeros(W1)
        fr[W2 + planes:] = zeros(W2)
        mid[1] = zeros(W2)

    for copy in g0:
        copy.wait()

    lab = ag[1, pl.ds(bx * s, ext // 4)]
    rate = lookup(lab, lambda r: rates[0, r])
    iv = 1.0 / (1.0 + 6.0 * rate)
    inv[...] = iv
    wt[...] = rate * iv
    src[...] = lookup(lab, lambda r: heat[n, r])

    lab_all = ag[1, pad:pad + cx]
    c_rate = FINE_STEPS * lookup(lab_all, lambda r: rates[0, r]) / 16.0
    c_inv = 1.0 / (1.0 + 6.0 * c_rate)
    c_weight = c_rate * c_inv

    def advance(m, c):
        source = FINE_STEPS * lookup(lab_all, lambda r: heat[m, r])
        return c_jacobi((c + source) * c_inv, c, c_weight)

    own_c = lax.fori_loop(0, n, advance, ag[0, pad:pad + cx])
    dcur[...] = advance(n, own_c)
    kp[pad:pad + cx] = own_c

    @pl.when(first_slice)
    def _():
        @pl.when(has_hi)
        def _():
            ih_lo_wait = remote(init, t0.at[pl.ds(W1 + planes, W1)], ih_ss.at[0], ih_rs.at[0], (n, s + 1))
            ih_lo_wait.wait_recv()

        @pl.when(has_lo)
        def _():
            ih_hi_wait = remote(init, t0.at[pl.ds(0, W1)], ih_ss.at[1], ih_rs.at[1], (n, s - 1))
            ih_hi_wait.wait_recv()

        def lay(p, _):
            u[1 + p] = t0[p]
            u[1 + W1 + planes + p] = t0[W1 + planes + p]
            return 0
        lax.fori_loop(0, W1, lay, 0)

        def lay_own(p, _):
            u[1 + W1 + p] = init[p]
            return 0
        lax.fori_loop(0, planes, lay_own, 0)

    @pl.when(has_prev)
    def _():
        def lay(k, _):
            f = kp[bx * s + k]
            for r in range(4):
                for q in range(tiles):
                    u[1 + 4 * k + r, q] = f
            return 0
        lax.fori_loop(0, ext // 4, lay, 0)

    fine_step(0, ext, SWEEPS)
    fine_step(SWEEPS, ext - 2 * SWEEPS, SWEEPS)

    own_g = pl.ds(bx * s, bx)

    def coarse_part(stage, plane_of):
        for k in range(bx):
            gag[stage, bx * s + k] = restrict([plane_of(4 * k + r) for r in range(4)])
        copies = gather_start(stage + 1, gag.at[stage], lambda r: r.at[own_g])
        return copies

    def keep(p, _):
        fs[p] = u[1 + W1 + p]
        return 0
    lax.fori_loop(0, planes, keep, 0)
    g1 = coarse_part(0, lambda p: fs[p])

    f_own = remote(fs, fr.at[pl.ds(W2, planes)], f_ss.at[0], f_rs.at[0], (n + 1, s))
    f_lo = remote(fs.at[pl.ds(0, W2)], fr.at[pl.ds(W2 + planes, W2)], f_ss.at[1], f_rs.at[1], (n + 1, s - 1))
    f_hi = remote(fs.at[pl.ds(planes - W2, W2)], fr.at[pl.ds(0, W2)], f_ss.at[2], f_rs.at[2], (n + 1, s + 1))

    @pl.when(has_next)
    def _():
        f_own.start()

    @pl.when(has_next & has_lo)
    def _():
        f_lo.start()

    @pl.when(has_next & has_hi)
    def _():
        f_hi.start()

    for copy in g1:
        copy.wait()

    def chain(stage):
        e_copy = remote(es.at[stage], er.at[stage], e_ss.at[stage], e_rs.at[stage], (n + 1, s))

        @pl.when(first_slice)
        def _():
            er[stage] = jnp.zeros((cx, cy, lanes), F32)

        @pl.when(has_prev)
        def _():
            e_copy.wait_recv()
        e = er[stage]
        corr = c_jacobi(e * c_inv, e, c_weight)
        rf = gag[stage]
        es[stage] = corr + (rf - dcur[...])

        @pl.when(has_next)
        def _():
            e_copy.start()
        dcur[...] = rf + corr
        return corr

    cs[...] = chain(0)
    c_copy = remote(cs, cr, c_ss, c_rs, (n + 1, s))

    @pl.when(has_next)
    def _():
        c_copy.start()

    off = W1 - W2
    span = planes + 2 * W2

    @pl.when(first_slice)
    def _():
        def lay(p, _):
            u[1 + off + p] = t0[off + p]
            u[1 + W1 + planes + p] = t0[W1 + planes + p]
            return 0
        lax.fori_loop(0, W2, lay, 0)

        def lay_own(p, _):
            u[1 + W1 + p] = init[p]
            return 0
        lax.fori_loop(0, planes, lay_own, 0)

    @pl.when(has_prev)
    def _():
        c_copy.wait_recv()
        f_own.wait_recv()

        @pl.when(has_hi)
        def _():
            f_lo.wait_recv()

        @pl.when(has_lo)
        def _():
            f_hi.wait_recv()
        kp[pad:pad + cx] = cr[...]

        def lay(k, _):
            f = kp[bx * s + off // 4 + k]
            for r in range(4):
                for q in range(tiles):
                    u[1 + off + 4 * k + r, q] = fr[4 * k + r, q] + f
            return 0
        lax.fori_loop(0, span // 4, lay, 0)

    fine_step(off, span, SWEEPS)

    m_lo = remote(u.at[pl.ds(1 + W1, W2)], mid.at[1], m_ss.at[0], m_rs.at[0], (n, s - 1))
    m_hi = remote(u.at[pl.ds(1 + W1 + planes - W2, W2)], mid.at[0], m_ss.at[1], m_rs.at[1], (n, s + 1))

    @pl.when(has_lo)
    def _():
        m_lo.start()

    @pl.when(has_hi)
    def _():
        m_hi.start()

    @pl.when(has_lo)
    def _():
        m_hi.wait_recv()
        m_lo.wait_send()

    @pl.when(has_hi)
    def _():
        m_lo.wait_recv()
        m_hi.wait_send()

    def lay_mid(p, _):
        u[1 + off + p] = mid[0, p]
        u[1 + W1 + planes + p] = mid[1, p]
        return 0
    lax.fori_loop(0, W2, lay_mid, 0)
    fine_step(off, span, SWEEPS)

    g2 = coarse_part(1, lambda p: u[1 + W1 + p])
    for copy in g2:
        copy.wait()
    kp[pad:pad + cx] = chain(1)

    from_tiles = jnp.where(zj == zs * (zi % lanes) + zi // lanes, F32(1.0), F32(0.0))

    rows_from_tiles = jnp.where(yi == ts * (yj % cy) + yj // cy, F32(1.0), F32(0.0))

    def finish(p, _):
        f = kp[pad + bx * s + p // 4]
        w = u[1 + W1 + p]
        rows = jnp.concatenate(
            [jnp.concatenate([w[t * zs + c] + f for c in range(zs)], 1) for t in range(ts)], 0)
        out[0, p] = dot(rows_from_tiles, dot(rows, from_tiles))
        return 0
    lax.fori_loop(0, planes, finish, 0, unroll=2)

    @pl.when(first_slice & has_lo)
    def _():
        ih_lo.wait_send()

    @pl.when(first_slice & has_hi)
    def _():
        ih_hi.wait_send()

    @pl.when(has_next)
    def _():
        f_own.wait_send()
        c_copy.wait_send()
        for stage in range(2):
            remote(es.at[stage], er.at[stage], e_ss.at[stage], e_rs.at[stage], (n + 1, s)).wait_send()

    @pl.when(has_next & has_lo)
    def _():
        f_lo.wait_send()

    @pl.when(has_next & has_hi)
    def _():
        f_hi.wait_send()


def solution(mesh):
    n_count, s_count = mesh.shape["tm"], mesh.shape["space"]

    def on_device(init, labels, rates, heat):
        planes, ny, nz = init.shape
        bx, cy, cz = labels.shape
        cx = bx * s_count
        lanes = 128
        tile = (ny * nz // (cy * lanes), cy, lanes)
        pad = W1 // 4
        ext = planes + 2 * W1
        dma = pltpu.SemaphoreType.DMA

        def vm(*shape):
            return pltpu.VMEM(shape, F32)

        vmem = pl.BlockSpec(memory_space=pltpu.VMEM)
        return pl.pallas_call(
            functools.partial(kernel, n_count, s_count),
            out_shape=jax.ShapeDtypeStruct((1, planes, ny, nz), F32),
            in_specs=[pl.BlockSpec(memory_space=pl.ANY)] * 4,
            out_specs=vmem,
            scratch_shapes=[
                vm(*init.shape), pltpu.VMEM(labels.shape, labels.dtype),
                pltpu.SMEM((1, rates.shape[0]), F32), pltpu.SMEM(heat.shape, F32),
                dma((4,)), vm(planes, *tile),
                vm(2, cx + 2 * pad, cy, lanes),
                vm(2, cx, cy, lanes),
                vm(ext, *tile),
                vm(ext + 2, *tile),
                vm(ext, *tile), vm(ext // 4, cy, lanes), vm(ext // 4, cy, lanes), vm(ext // 4, cy, lanes),
                vm(planes, *tile),
                vm(planes + 2 * W2, *tile),
                vm(2, W2, *tile),
                vm(cx + 2 * pad, cy, lanes),
                vm(2, cx, cy, lanes), vm(2, cx, cy, lanes),
                vm(cx, cy, lanes), vm(cx, cy, lanes), vm(cx, cy, lanes),
                dma((3, s_count)), dma((3, s_count)),
                dma((2,)), dma((2,)),
                dma((3,)), dma((3,)),
                dma((2,)), dma((2,)),
                dma((2,)), dma((2,)),
                dma(()), dma(()),
            ],
            compiler_params=pltpu.CompilerParams(
                collective_id=0, has_side_effects=True, vmem_limit_bytes=48 * 1024 * 1024),
            name="parareal",
        )(init, labels, rates.reshape(1, -1), heat)

    return jax.shard_map(
        on_device,
        mesh=mesh,
        in_specs=(P("space", None, None), P("space", None, None), P(), P()),
        out_specs=P("tm", "space", None, None),
        check_vma=False,
    )
```

```python
import functools

import jax
import jax.numpy as jnp
from jax import lax
from jax.experimental import pallas as pl
from jax.experimental.pallas import tpu as pltpu
from jax.sharding import PartitionSpec as P

FINE_STEPS = 2
SWEEPS = 8
C_SWEEPS = 4
W1 = FINE_STEPS * SWEEPS
EW = 2 * W1
F32 = jnp.float32
MESH = pl.DeviceIdType.MESH
HI = lax.Precision.HIGHEST


def dot(a, b):
    return jnp.dot(a, b, precision=HI, preferred_element_type=F32)


def kernel(
    n_count, s_count,
    init_hbm, labels_hbm, rates_hbm, heat_hbm,
    out,
    raw, labels, rates, heat, in_sem, init,
    ag, gag, t0, u, sc, wt, inv, src, fs, fr, kp, es, er, cs, cr, dcur,
    ag_ss, ag_rs, ih_ss, ih_rs, f_ss, f_rs, e_ss, e_rs, c_ss, c_rs,
):
    n = lax.axis_index("tm")
    s = lax.axis_index("space")
    planes, ny, nz = init_hbm.shape
    bx, cy, cz = labels_hbm.shape
    cx = bx * s_count
    lanes = ag.shape[-1]
    ts, zs = ny // cy, nz // lanes
    regions = rates_hbm.shape[1]
    pad = EW // 4
    has_prev, has_next = n > 0, n < n_count - 1
    has_lo, has_hi = s > 0, s < s_count - 1

    fetches = [pltpu.make_async_copy(a, b, in_sem.at[i]) for i, (a, b) in enumerate(
        ((init_hbm, raw), (labels_hbm, labels), (rates_hbm, rates), (heat_hbm, heat)))]
    for fetch in fetches:
        fetch.start()

    barrier = pltpu.get_barrier_semaphore()
    def greet(cond, dev):
        @pl.when(cond)
        def _():
            pl.semaphore_signal(barrier, inc=1, device_id=dev, device_id_type=MESH)
    def one(c):
        return jnp.where(c, 1, 0).astype(jnp.int32)
    for j in range(1, s_count):
        pl.semaphore_signal(
            barrier, inc=1, device_id=(n, lax.rem(s + j, s_count)), device_id_type=MESH)
    partners = s_count - 1
    for cond_n, dn in ((has_prev, -1), (has_next, 1)):
        edge = n == (1 if dn < 0 else 0)
        for cond_s, ds in ((None, 0), (has_lo, -1), (has_hi, 1)):
            cond = cond_n if cond_s is None else cond_n & cond_s & edge
            greet(cond, (n + dn, s + ds))
            partners = partners + one(cond)
    pl.semaphore_wait(barrier, partners)

    def remote(a, b, ss, rs, dev):
        return pltpu.make_async_remote_copy(
            src_ref=a, dst_ref=b, send_sem=ss, recv_sem=rs, device_id=dev, device_id_type=MESH)

    half = 4 // zs

    def restrict(planes4):
        total = planes4[0]
        for extra in planes4[1:]:
            total = total + extra
        part = total[0]
        for k in range(1, ts * zs):
            part = part + total[k]
        lane = lax.broadcasted_iota(jnp.int32, part.shape, 1)
        step = 1
        while step < half:
            swap = jnp.where(lane % (2 * step) < step,
                             pltpu.roll(part, lanes - step, 1), pltpu.roll(part, step, 1))
            part = part + swap
            step *= 2
        return part * F32(1.0 / 64.0)

    def lookup(lab, row):
        total = jnp.zeros(lab.shape, F32)
        for r in range(regions):
            total = total + jnp.where(lab == F32(r), row(r), F32(0.0))
        return total

    crow = lax.broadcasted_iota(jnp.int32, (cx, cy, lanes), 1)
    ccol = lax.broadcasted_iota(jnp.int32, (cx, cy, lanes), 2)
    c_first, c_last = crow == 0, crow == cy - 1
    cz_first, cz_last = ccol < half, ccol >= lanes - half
    czero = jnp.zeros((1, cy, lanes), F32)

    def c_neighbours(w):
        total = jnp.concatenate([czero, w[:-1]], 0) + jnp.concatenate([w[1:], czero], 0)
        total = total + (jnp.where(c_first, F32(0.0), pltpu.roll(w, 1, 1))
                         + jnp.where(c_last, F32(0.0), pltpu.roll(w, cy - 1, 1)))
        return total + (jnp.where(cz_first, F32(0.0), pltpu.roll(w, half, 2))
                        + jnp.where(cz_last, F32(0.0), pltpu.roll(w, lanes - half, 2)))

    def c_jacobi(scaled, w, c_weight):
        for _ in range(C_SWEEPS):
            w = scaled + c_weight * c_neighbours(w)
        return w

    row = lax.broadcasted_iota(jnp.int32, (cy, lanes), 0)
    col = lax.broadcasted_iota(jnp.int32, (cy, lanes), 1)
    y_first, y_last = row == 0, row == cy - 1
    z_first, z_last = col == 0, col == lanes - 1

    def in_plane(w, k):
        t, c = k // zs, k % zs
        if t > 0:
            a = w[k - zs]
        else:
            a = jnp.where(y_first, F32(0.0), pltpu.roll(w[(ts - 1) * zs + c], 1, 0))
        if t < ts - 1:
            b = w[k + zs]
        else:
            b = jnp.where(y_last, F32(0.0), pltpu.roll(w[c], cy - 1, 0))
        if c > 0:
            d = w[k - 1]
        else:
            d = jnp.where(z_first, F32(0.0), pltpu.roll(w[k + zs - 1], 1, 1))
        if c < zs - 1:
            e = w[k + 1]
        else:
            e = jnp.where(z_last, F32(0.0), pltpu.roll(w[k - zs + 1], lanes - 1, 1))
        return (a + b) + (d + e)

    tiles = ts * zs

    def fine_step(first, length, shrink):
        def scale(q, _):
            g = first // 4 + q
            iv, so = inv[g], src[g]
            for r in range(4):
                p = first + 4 * q + r
                for k in range(tiles):
                    sc[p, k] = (u[p + 1, k] + so) * iv
            return 0
        lax.fori_loop(0, length // 4, scale, 0)

        def sweep(i, _):
            cut = 4 * (i // 4)
            lo = first + cut

            def quad(q, carry):
                before, cur = carry
                we = wt[lo // 4 + q]
                for r in range(4):
                    p = lo + 4 * q + r
                    after = [u[p + 2, k] for k in range(tiles)]
                    for k in range(tiles):
                        u[p + 1, k] = sc[p, k] + we * ((before[k] + after[k]) + in_plane(cur, k))
                    before, cur = cur, after
                return before, cur

            lax.fori_loop(0, (length - 2 * cut) // 4, quad,
                          ([u[lo, k] for k in range(tiles)], [u[lo + 1, k] for k in range(tiles)]))
            return 0
        lax.fori_loop(0, shrink, sweep, 0)

    def gather_start(stage, ref, mine):
        copies = []
        for j in range(1, s_count):
            copy = remote(mine(ref), mine(ref), ag_ss.at[stage, j], ag_rs.at[stage, j],
                          (n, lax.rem(s + j, s_count)))
            copy.start()
            copies.append(copy)
        return copies

    own = pl.ds(pad + bx * s, bx)

    ext = EW * 2 + planes
    span = W1 * 2 + planes
    off = EW - W1
    zero_block = jnp.zeros((pad, cy, lanes), F32)
    for k in (0, pad + cx):
        ag[0, k:k + pad] = zero_block
        ag[1, k:k + pad] = zero_block - 1.0
        kp[k:k + pad] = zero_block
    def zeros(*lead):
        return jnp.zeros(lead + (tiles, cy, lanes), F32)

    zero_fine = zeros()
    u[0] = zero_fine
    u[ext + 1] = zero_fine

    for fetch in fetches:
        fetch.wait()

    zi = lax.broadcasted_iota(jnp.int32, (nz, nz), 0)
    zj = lax.broadcasted_iota(jnp.int32, (nz, nz), 1)
    to_tiles = jnp.where(zi == zs * (zj % lanes) + zj // lanes, F32(1.0), F32(0.0))

    yi = lax.broadcasted_iota(jnp.int32, (ny, ny), 0)
    yj = lax.broadcasted_iota(jnp.int32, (ny, ny), 1)
    rows_to_tiles = jnp.where(yj == ts * (yi % cy) + yi // cy, F32(1.0), F32(0.0))

    def load(p, _):
        moved = dot(rows_to_tiles, dot(raw[p], to_tiles))
        for t in range(ts):
            for c in range(zs):
                init[p, t * zs + c] = moved[t * cy:(t + 1) * cy, c * lanes:(c + 1) * lanes]
        return 0
    lax.fori_loop(0, planes, load, 0, unroll=2)

    li = lax.broadcasted_iota(jnp.int32, (cz, lanes), 0)
    lj = lax.broadcasted_iota(jnp.int32, (cz, lanes), 1)
    spread = jnp.where(li == lj // half, F32(1.0), F32(0.0))
    for k in range(bx):
        ag[0, pad + bx * s + k] = restrict([init[4 * k + r] for r in range(4)])
        ag[1, pad + bx * s + k] = dot(labels[k].astype(F32), spread)
    g0 = gather_start(0, ag, lambda r: r.at[:, own])

    first_slice = n == 0
    ih_lo = remote(init, t0.at[pl.ds(W1 + planes, W1)], ih_ss.at[0], ih_rs.at[0], (n, s - 1))
    ih_hi = remote(init, t0.at[pl.ds(0, W1)], ih_ss.at[1], ih_rs.at[1], (n, s + 1))

    @pl.when(first_slice & has_lo)
    def _():
        ih_lo.start()

    @pl.when(first_slice & has_hi)
    def _():
        ih_hi.start()

    second_slice = n == 1

    @pl.when(first_slice & jnp.logical_not(has_lo))
    def _():
        t0[0:W1] = zeros(W1)

    @pl.when(first_slice & jnp.logical_not(has_hi))
    def _():
        t0[W1 + planes:] = zeros(W1)

    @pl.when(second_slice & jnp.logical_not(has_lo))
    def _():
        fr[0:W1] = zeros(W1)

    @pl.when(second_slice & jnp.logical_not(has_hi))
    def _():
        fr[W1 + planes:] = zeros(W1)

    for copy in g0:
        copy.wait()

    lab = ag[1, pl.ds(bx * s, ext // 4)]
    rate = lookup(lab, lambda r: rates[0, r])
    iv = 1.0 / (1.0 + 6.0 * rate)
    inv[...] = iv
    wt[...] = rate * iv
    src[...] = lookup(lab, lambda r: heat[n, r])

    lab_all = ag[1, pad:pad + cx]
    c_rate = FINE_STEPS * lookup(lab_all, lambda r: rates[0, r]) / 16.0
    c_inv = 1.0 / (1.0 + 6.0 * c_rate)
    c_weight = c_rate * c_inv

    def advance(m, c):
        source = FINE_STEPS * lookup(lab_all, lambda r: heat[m, r])
        return c_jacobi((c + source) * c_inv, c, c_weight)

    own_c = lax.fori_loop(0, n, advance, ag[0, pad:pad + cx])
    dcur[...] = advance(n, own_c)
    kp[pad:pad + cx] = own_c

    @pl.when(first_slice)
    def _():
        @pl.when(has_hi)
        def _():
            ih_lo_wait = remote(init, t0.at[pl.ds(W1 + planes, W1)], ih_ss.at[0], ih_rs.at[0], (n, s + 1))
            ih_lo_wait.wait_recv()

        @pl.when(has_lo)
        def _():
            ih_hi_wait = remote(init, t0.at[pl.ds(0, W1)], ih_ss.at[1], ih_rs.at[1], (n, s - 1))
            ih_hi_wait.wait_recv()

        def lay(p, _):
            u[1 + off + p] = t0[p]
            u[1 + EW + planes + p] = t0[W1 + planes + p]
            return 0
        lax.fori_loop(0, W1, lay, 0)
        u[off] = zero_fine
        u[off + span + 1] = zero_fine

        def lay_own(p, _):
            u[1 + EW + p] = init[p]
            return 0
        lax.fori_loop(0, planes, lay_own, 0)

    @pl.when(has_prev)
    def _():
        def lay(k, _):
            f = kp[bx * s + k]
            for r in range(4):
                for q in range(tiles):
                    u[1 + 4 * k + r, q] = f
            return 0
        lax.fori_loop(0, ext // 4, lay, 0)

    begin = jnp.where(first_slice, off, 0)
    size = jnp.where(first_slice, span, ext)
    fine_step(begin, size, SWEEPS)
    fine_step(begin + SWEEPS, size - 2 * SWEEPS, SWEEPS)

    own_g = pl.ds(bx * s, bx)

    def coarse_part(stage, plane_of):
        for k in range(bx):
            gag[stage, bx * s + k] = restrict([plane_of(4 * k + r) for r in range(4)])
        copies = gather_start(stage + 1, gag.at[stage], lambda r: r.at[own_g])
        return copies

    g1 = coarse_part(0, lambda p: u[1 + EW + p])

    def keep(p, _):
        fs[p] = u[1 + off + p]
        return 0
    lax.fori_loop(0, span, keep, 0)

    own_part = pl.ds(W1, planes)
    f_all = remote(fs, fr, f_ss.at[0], f_rs.at[0], (n + 1, s))
    f_own = remote(fs.at[own_part], fr.at[own_part], f_ss.at[0], f_rs.at[0], (n + 1, s))
    f_lo = remote(fs.at[own_part], fr.at[pl.ds(W1 + planes, W1)], f_ss.at[1], f_rs.at[1], (n + 1, s - 1))
    f_hi = remote(fs.at[own_part], fr.at[pl.ds(0, W1)], f_ss.at[2], f_rs.at[2], (n + 1, s + 1))

    @pl.when(first_slice & has_lo)
    def _():
        f_lo.start()

    @pl.when(first_slice & has_hi)
    def _():
        f_hi.start()

    @pl.when(first_slice & has_next)
    def _():
        f_own.start()

    @pl.when(has_prev & has_next)
    def _():
        f_all.start()

    for copy in g1:
        copy.wait()

    def chain(stage):
        e_copy = remote(es.at[stage], er.at[stage], e_ss.at[stage], e_rs.at[stage], (n + 1, s))

        @pl.when(first_slice)
        def _():
            er[stage] = jnp.zeros((cx, cy, lanes), F32)

        @pl.when(has_prev)
        def _():
            e_copy.wait_recv()
        e = er[stage]
        corr = c_jacobi(e * c_inv, e, c_weight)
        rf = gag[stage]
        es[stage] = corr + (rf - dcur[...])

        @pl.when(has_next)
        def _():
            e_copy.start()
        dcur[...] = rf + corr
        return corr

    cs[...] = chain(0)
    c_copy = remote(cs, cr, c_ss, c_rs, (n + 1, s))

    @pl.when(has_next)
    def _():
        c_copy.start()

    @pl.when(second_slice)
    def _():
        f_own.wait_recv()

        @pl.when(has_hi)
        def _():
            f_lo.wait_recv()

        @pl.when(has_lo)
        def _():
            f_hi.wait_recv()

    @pl.when(n > 1)
    def _():
        f_all.wait_recv()

    @pl.when(has_prev)
    def _():
        c_copy.wait_recv()
        kp[pad:pad + cx] = cr[...]

        def lay(k, _):
            f = kp[bx * s + off // 4 + k]
            for r in range(4):
                for q in range(tiles):
                    u[1 + off + 4 * k + r, q] = fr[4 * k + r, q] + f
            return 0
        lax.fori_loop(0, span // 4, lay, 0)
        fine_step(off, span, SWEEPS)
        fine_step(off + SWEEPS, span - 2 * SWEEPS, SWEEPS)

    g2 = coarse_part(1, lambda p: u[1 + EW + p])
    for copy in g2:
        copy.wait()
    kp[pad:pad + cx] = chain(1)

    from_tiles = jnp.where(zj == zs * (zi % lanes) + zi // lanes, F32(1.0), F32(0.0))

    rows_from_tiles = jnp.where(yi == ts * (yj % cy) + yj // cy, F32(1.0), F32(0.0))

    def finish(p, _):
        f = kp[pad + bx * s + p // 4]
        w = u[1 + EW + p]
        rows = jnp.concatenate(
            [jnp.concatenate([w[t * zs + c] + f for c in range(zs)], 1) for t in range(ts)], 0)
        out[0, p] = dot(rows_from_tiles, dot(rows, from_tiles))
        return 0
    lax.fori_loop(0, planes, finish, 0, unroll=2)

    @pl.when(first_slice & has_lo)
    def _():
        ih_lo.wait_send()

    @pl.when(first_slice & has_hi)
    def _():
        ih_hi.wait_send()

    @pl.when(has_next)
    def _():
        c_copy.wait_send()
        for stage in range(2):
            remote(es.at[stage], er.at[stage], e_ss.at[stage], e_rs.at[stage], (n + 1, s)).wait_send()

    @pl.when(has_prev & has_next)
    def _():
        f_all.wait_send()

    @pl.when(first_slice & has_next)
    def _():
        f_own.wait_send()

    @pl.when(first_slice & has_lo)
    def _():
        f_lo.wait_send()

    @pl.when(first_slice & has_hi)
    def _():
        f_hi.wait_send()


def solution(mesh):
    n_count, s_count = mesh.shape["tm"], mesh.shape["space"]

    def on_device(init, labels, rates, heat):
        planes, ny, nz = init.shape
        bx, cy, cz = labels.shape
        cx = bx * s_count
        lanes = 128
        tile = (ny * nz // (cy * lanes), cy, lanes)
        pad = EW // 4
        ext = planes + 2 * EW
        span = planes + 2 * W1
        dma = pltpu.SemaphoreType.DMA

        def vm(*shape):
            return pltpu.VMEM(shape, F32)

        vmem = pl.BlockSpec(memory_space=pltpu.VMEM)
        return pl.pallas_call(
            functools.partial(kernel, n_count, s_count),
            out_shape=jax.ShapeDtypeStruct((1, planes, ny, nz), F32),
            in_specs=[pl.BlockSpec(memory_space=pl.ANY)] * 4,
            out_specs=vmem,
            scratch_shapes=[
                vm(*init.shape), pltpu.VMEM(labels.shape, labels.dtype),
                pltpu.SMEM((1, rates.shape[0]), F32), pltpu.SMEM(heat.shape, F32),
                dma((4,)), vm(planes, *tile),
                vm(2, cx + 2 * pad, cy, lanes),
                vm(2, cx, cy, lanes),
                vm(span, *tile),
                vm(ext + 2, *tile),
                vm(ext, *tile), vm(ext // 4, cy, lanes), vm(ext // 4, cy, lanes), vm(ext // 4, cy, lanes),
                vm(span, *tile),
                vm(span, *tile),
                vm(cx + 2 * pad, cy, lanes),
                vm(2, cx, cy, lanes), vm(2, cx, cy, lanes),
                vm(cx, cy, lanes), vm(cx, cy, lanes), vm(cx, cy, lanes),
                dma((3, s_count)), dma((3, s_count)),
                dma((2,)), dma((2,)),
                dma((3,)), dma((3,)),
                dma((2,)), dma((2,)),
                dma(()), dma(()),
            ],
            compiler_params=pltpu.CompilerParams(
                collective_id=0, has_side_effects=True, vmem_limit_bytes=48 * 1024 * 1024),
            name="parareal",
        )(init, labels, rates.reshape(1, -1), heat)

    return jax.shard_map(
        on_device,
        mesh=mesh,
        in_specs=(P("space", None, None), P("space", None, None), P(), P()),
        out_specs=P("tm", "space", None, None),
        check_vma=False,
    )
```

```python
import functools

import jax
import jax.numpy as jnp
from jax import lax
from jax.experimental import pallas as pl
from jax.experimental.pallas import tpu as pltpu
from jax.sharding import PartitionSpec as P

FINE_STEPS = 2
SWEEPS = 8
C_SWEEPS = 4
W1 = FINE_STEPS * SWEEPS
W2 = SWEEPS
F32 = jnp.float32
BF16 = jnp.bfloat16
MESH = pl.DeviceIdType.MESH
HI = lax.Precision.HIGHEST


def dot(a, b):
    return jnp.dot(a, b, precision=HI, preferred_element_type=F32)


def kernel(
    n_count, s_count,
    init_hbm, labels_hbm, rates_hbm, heat_hbm,
    out,
    raw, labels, rates, heat, in_sem, init,
    ag, gag, t0, u, sc, wt, inv, src, fs, fr, mid, kp, es, er, cs, cr, dcur,
    ag_ss, ag_rs, ih_ss, ih_rs, f_ss, f_rs, m_ss, m_rs, e_ss, e_rs, c_ss, c_rs,
):
    n = lax.axis_index("tm")
    s = lax.axis_index("space")
    planes, ny, nz = init_hbm.shape
    bx, cy, cz = labels_hbm.shape
    cx = bx * s_count
    lanes = ag.shape[-1]
    ts, zs = ny // cy, nz // lanes
    regions = rates_hbm.shape[1]
    pad = W1 // 4
    has_prev, has_next = n > 0, n < n_count - 1
    has_lo, has_hi = s > 0, s < s_count - 1

    pairs = [(labels_hbm, labels), (rates_hbm, rates), (heat_hbm, heat)]
    pairs += [(init_hbm.at[:, :, pl.ds(c * lanes, lanes)], raw.at[c]) for c in range(zs)]
    fetches = [pltpu.make_async_copy(a, b, in_sem.at[i]) for i, (a, b) in enumerate(pairs)]
    for fetch in fetches:
        fetch.start()

    barrier = pltpu.get_barrier_semaphore()
    def greet(cond, dev):
        @pl.when(cond)
        def _():
            pl.semaphore_signal(barrier, inc=1, device_id=dev, device_id_type=MESH)
    def one(c):
        return jnp.where(c, 1, 0).astype(jnp.int32)
    for j in range(1, s_count):
        pl.semaphore_signal(
            barrier, inc=1, device_id=(n, lax.rem(s + j, s_count)), device_id_type=MESH)
    partners = s_count - 1
    for cond_n, dn in ((has_prev, -1), (has_next, 1)):
        for cond_s, ds in ((None, 0), (has_lo, -1), (has_hi, 1)):
            cond = cond_n if cond_s is None else cond_n & cond_s
            greet(cond, (n + dn, s + ds))
            partners = partners + one(cond)
    pl.semaphore_wait(barrier, partners)

    def remote(a, b, ss, rs, dev):
        return pltpu.make_async_remote_copy(
            src_ref=a, dst_ref=b, send_sem=ss, recv_sem=rs, device_id=dev, device_id_type=MESH)

    half = 4 // zs

    def restrict(planes4):
        total = planes4[0]
        for extra in planes4[1:]:
            total = total + extra
        part = total[0]
        for k in range(1, ts * zs):
            part = part + total[k]
        lane = lax.broadcasted_iota(jnp.int32, part.shape, 1)
        step = 1
        while step < half:
            swap = jnp.where(lane % (2 * step) < step,
                             pltpu.roll(part, lanes - step, 1), pltpu.roll(part, step, 1))
            part = part + swap
            step *= 2
        return part * F32(1.0 / 64.0)

    def lookup(lab, row):
        total = jnp.zeros(lab.shape, F32)
        for r in range(regions):
            total = total + jnp.where(lab == F32(r), row(r), F32(0.0))
        return total

    crow = lax.broadcasted_iota(jnp.int32, (cx, cy, lanes), 1)
    ccol = lax.broadcasted_iota(jnp.int32, (cx, cy, lanes), 2)
    c_first, c_last = crow == 0, crow == cy - 1
    cz_first, cz_last = ccol < half, ccol >= lanes - half
    czero = jnp.zeros((1, cy, lanes), F32)

    def c_neighbours(w):
        total = jnp.concatenate([czero, w[:-1]], 0) + jnp.concatenate([w[1:], czero], 0)
        total = total + (jnp.where(c_first, F32(0.0), pltpu.roll(w, 1, 1))
                         + jnp.where(c_last, F32(0.0), pltpu.roll(w, cy - 1, 1)))
        return total + (jnp.where(cz_first, F32(0.0), pltpu.roll(w, half, 2))
                        + jnp.where(cz_last, F32(0.0), pltpu.roll(w, lanes - half, 2)))

    def c_jacobi(scaled, w, c_weight):
        for _ in range(C_SWEEPS):
            w = scaled + c_weight * c_neighbours(w)
        return w

    row = lax.broadcasted_iota(jnp.int32, (cy, lanes), 0)
    col = lax.broadcasted_iota(jnp.int32, (cy, lanes), 1)
    y_first, y_last = row == 0, row == cy - 1
    z_first, z_last = col == 0, col == lanes - 1

    def in_plane(w, k):
        t, c = k // zs, k % zs
        if t > 0:
            a = w[k - zs]
        else:
            a = jnp.where(y_first, F32(0.0), pltpu.roll(w[(ts - 1) * zs + c], 1, 0))
        if t < ts - 1:
            b = w[k + zs]
        else:
            b = jnp.where(y_last, F32(0.0), pltpu.roll(w[c], cy - 1, 0))
        if c > 0:
            d = w[k - 1]
        else:
            d = jnp.where(z_first, F32(0.0), pltpu.roll(w[k + zs - 1], 1, 1))
        if c < zs - 1:
            e = w[k + 1]
        else:
            e = jnp.where(z_last, F32(0.0), pltpu.roll(w[k - zs + 1], lanes - 1, 1))
        return (a + b) + (d + e)

    tiles = ts * zs

    def fine_step(first, length, shrink):
        def scale(q, _):
            g = first // 4 + q
            iv, so = inv[g], src[g]
            for r in range(4):
                p = first + 4 * q + r
                for k in range(tiles):
                    sc[p, k] = (u[p + 1, k] + so) * iv
            return 0
        lax.fori_loop(0, length // 4, scale, 0)

        def sweep(i, _):
            cut = 4 * (i // 4)
            lo = first + cut

            def quad(q, carry):
                before, cur = carry
                we = wt[lo // 4 + q]
                for r in range(4):
                    p = lo + 4 * q + r
                    after = [u[p + 2, k] for k in range(tiles)]
                    for k in range(tiles):
                        u[p + 1, k] = sc[p, k] + we * ((before[k] + after[k]) + in_plane(cur, k))
                    before, cur = cur, after
                return before, cur

            lax.fori_loop(0, (length - 2 * cut) // 4, quad,
                          ([u[lo, k] for k in range(tiles)], [u[lo + 1, k] for k in range(tiles)]))
            return 0
        lax.fori_loop(0, shrink, sweep, 0)

    def gather_start(stage, ref, mine):
        copies = []
        for j in range(1, s_count):
            copy = remote(mine(ref), mine(ref), ag_ss.at[stage, j], ag_rs.at[stage, j],
                          (n, lax.rem(s + j, s_count)))
            copy.start()
            copies.append(copy)
        return copies

    own = pl.ds(pad + bx * s, bx)

    ext = W1 * 2 + planes
    zero_block = jnp.zeros((pad, cy, lanes), F32)
    for k in (0, pad + cx):
        ag[0, k:k + pad] = zero_block
        ag[1, k:k + pad] = zero_block - 1.0
        kp[k:k + pad] = zero_block
    def zeros(*lead):
        return jnp.zeros(lead + (tiles, cy, lanes), F32)

    zero_fine = zeros()
    u[0] = zero_fine
    u[ext + 1] = zero_fine

    for fetch in fetches:
        fetch.wait()

    zi = lax.broadcasted_iota(jnp.int32, (nz, nz), 0)
    zj = lax.broadcasted_iota(jnp.int32, (nz, nz), 1)
    to_tiles = jnp.where(zi == zs * (zj % lanes) + zj // lanes, F32(1.0), F32(0.0)).astype(BF16)
    from_tiles = jnp.where(zj == zs * (zi % lanes) + zi // lanes, F32(1.0), F32(0.0)).astype(BF16)

    def permute(rows, one_hot):
        high = rows.astype(BF16)
        rest = rows - high.astype(F32)
        middle = rest.astype(BF16)
        low = (rest - middle.astype(F32)).astype(BF16)
        parts = [jnp.dot(x, one_hot, preferred_element_type=F32) for x in (high, middle, low)]
        return (parts[0] + parts[1]) + parts[2]

    def load(q, _):
        rows = jnp.concatenate([
            jnp.concatenate([raw[c, 4 * q + r, pl.ds(t, cy, stride=ts), :] for c in range(zs)], 1)
            for r in range(4) for t in range(ts)], 0)
        moved = permute(rows, to_tiles)
        for r in range(4):
            for t in range(ts):
                for c in range(zs):
                    at = (r * ts + t) * cy
                    init[4 * q + r, t * zs + c] = moved[at:at + cy, c * lanes:(c + 1) * lanes]
        return 0
    lax.fori_loop(0, bx, load, 0)

    li = lax.broadcasted_iota(jnp.int32, (cz, lanes), 0)
    lj = lax.broadcasted_iota(jnp.int32, (cz, lanes), 1)
    spread = jnp.where(li == lj // half, F32(1.0), F32(0.0))
    for k in range(bx):
        ag[0, pad + bx * s + k] = restrict([init[4 * k + r] for r in range(4)])
        ag[1, pad + bx * s + k] = dot(labels[k].astype(F32), spread)
    g0 = gather_start(0, ag, lambda r: r.at[:, own])

    first_slice = n == 0
    ih_lo = remote(init, t0.at[pl.ds(W1 + planes, W1)], ih_ss.at[0], ih_rs.at[0], (n, s - 1))
    ih_hi = remote(init, t0.at[pl.ds(0, W1)], ih_ss.at[1], ih_rs.at[1], (n, s + 1))

    @pl.when(first_slice & has_lo)
    def _():
        ih_lo.start()

    @pl.when(first_slice & has_hi)
    def _():
        ih_hi.start()

    @pl.when(jnp.logical_not(has_lo))
    def _():
        t0[0:W1] = zeros(W1)
        fr[0:W2] = zeros(W2)
        mid[0] = zeros(W2)

    @pl.when(jnp.logical_not(has_hi))
    def _():
        t0[W1 + planes:] = zeros(W1)
        fr[W2 + planes:] = zeros(W2)
        mid[1] = zeros(W2)

    for copy in g0:
        copy.wait()

    lab = ag[1, pl.ds(bx * s, ext // 4)]
    rate = lookup(lab, lambda r: rates[0, r])
    iv = 1.0 / (1.0 + 6.0 * rate)
    inv[...] = iv
    wt[...] = rate * iv
    src[...] = lookup(lab, lambda r: heat[n, r])

    lab_all = ag[1, pad:pad + cx]
    c_rate = FINE_STEPS * lookup(lab_all, lambda r: rates[0, r]) / 16.0
    c_inv = 1.0 / (1.0 + 6.0 * c_rate)
    c_weight = c_rate * c_inv

    def advance(m, c):
        source = FINE_STEPS * lookup(lab_all, lambda r: heat[m, r])
        return c_jacobi((c + source) * c_inv, c, c_weight)

    own_c = lax.fori_loop(0, n, advance, ag[0, pad:pad + cx])
    dcur[...] = advance(n, own_c)
    kp[pad:pad + cx] = own_c

    @pl.when(first_slice)
    def _():
        @pl.when(has_hi)
        def _():
            ih_lo_wait = remote(init, t0.at[pl.ds(W1 + planes, W1)], ih_ss.at[0], ih_rs.at[0], (n, s + 1))
            ih_lo_wait.wait_recv()

        @pl.when(has_lo)
        def _():
            ih_hi_wait = remote(init, t0.at[pl.ds(0, W1)], ih_ss.at[1], ih_rs.at[1], (n, s - 1))
            ih_hi_wait.wait_recv()

        def lay(p, _):
            u[1 + p] = t0[p]
            u[1 + W1 + planes + p] = t0[W1 + planes + p]
            return 0
        lax.fori_loop(0, W1, lay, 0)

        def lay_own(p, _):
            u[1 + W1 + p] = init[p]
            return 0
        lax.fori_loop(0, planes, lay_own, 0)

    @pl.when(has_prev)
    def _():
        def lay(k, _):
            f = kp[bx * s + k]
            for r in range(4):
                for q in range(tiles):
                    u[1 + 4 * k + r, q] = f
            return 0
        lax.fori_loop(0, ext // 4, lay, 0)

    fine_step(0, ext, SWEEPS)
    fine_step(SWEEPS, ext - 2 * SWEEPS, SWEEPS)

    own_g = pl.ds(bx * s, bx)

    def coarse_part(stage, plane_of):
        for k in range(bx):
            gag[stage, bx * s + k] = restrict([plane_of(4 * k + r) for r in range(4)])
        copies = gather_start(stage + 1, gag.at[stage], lambda r: r.at[own_g])
        return copies

    def keep(p, _):
        fs[p] = u[1 + W1 + p]
        return 0
    lax.fori_loop(0, planes, keep, 0)
    g1 = coarse_part(0, lambda p: fs[p])

    f_own = remote(fs, fr.at[pl.ds(W2, planes)], f_ss.at[0], f_rs.at[0], (n + 1, s))
    f_lo = remote(fs.at[pl.ds(0, W2)], fr.at[pl.ds(W2 + planes, W2)], f_ss.at[1], f_rs.at[1], (n + 1, s - 1))
    f_hi = remote(fs.at[pl.ds(planes - W2, W2)], fr.at[pl.ds(0, W2)], f_ss.at[2], f_rs.at[2], (n + 1, s + 1))

    @pl.when(has_next)
    def _():
        f_own.start()

    @pl.when(has_next & has_lo)
    def _():
        f_lo.start()

    @pl.when(has_next & has_hi)
    def _():
        f_hi.start()

    for copy in g1:
        copy.wait()

    def chain(stage):
        e_copy = remote(es.at[stage], er.at[stage], e_ss.at[stage], e_rs.at[stage], (n + 1, s))

        @pl.when(first_slice)
        def _():
            er[stage] = jnp.zeros((cx, cy, lanes), F32)

        @pl.when(has_prev)
        def _():
            e_copy.wait_recv()
        e = er[stage]
        corr = c_jacobi(e * c_inv, e, c_weight)
        rf = gag[stage]
        es[stage] = corr + (rf - dcur[...])

        @pl.when(has_next)
        def _():
            e_copy.start()
        dcur[...] = rf + corr
        return corr

    cs[...] = chain(0)
    c_copy = remote(cs, cr, c_ss, c_rs, (n + 1, s))

    @pl.when(has_next)
    def _():
        c_copy.start()

    off = W1 - W2
    span = planes + 2 * W2

    @pl.when(first_slice)
    def _():
        def lay(p, _):
            u[1 + off + p] = t0[off + p]
            u[1 + W1 + planes + p] = t0[W1 + planes + p]
            return 0
        lax.fori_loop(0, W2, lay, 0)

        def lay_own(p, _):
            u[1 + W1 + p] = init[p]
            return 0
        lax.fori_loop(0, planes, lay_own, 0)

    @pl.when(has_prev)
    def _():
        c_copy.wait_recv()
        f_own.wait_recv()

        @pl.when(has_hi)
        def _():
            f_lo.wait_recv()

        @pl.when(has_lo)
        def _():
            f_hi.wait_recv()
        kp[pad:pad + cx] = cr[...]

        def lay(k, _):
            f = kp[bx * s + off // 4 + k]
            for r in range(4):
                for q in range(tiles):
                    u[1 + off + 4 * k + r, q] = fr[4 * k + r, q] + f
            return 0
        lax.fori_loop(0, span // 4, lay, 0)

    fine_step(off, span, SWEEPS)

    m_lo = remote(u.at[pl.ds(1 + W1, W2)], mid.at[1], m_ss.at[0], m_rs.at[0], (n, s - 1))
    m_hi = remote(u.at[pl.ds(1 + W1 + planes - W2, W2)], mid.at[0], m_ss.at[1], m_rs.at[1], (n, s + 1))

    @pl.when(has_lo)
    def _():
        m_lo.start()

    @pl.when(has_hi)
    def _():
        m_hi.start()

    @pl.when(has_lo)
    def _():
        m_hi.wait_recv()
        m_lo.wait_send()

    @pl.when(has_hi)
    def _():
        m_lo.wait_recv()
        m_hi.wait_send()

    def lay_mid(p, _):
        u[1 + off + p] = mid[0, p]
        u[1 + W1 + planes + p] = mid[1, p]
        return 0
    lax.fori_loop(0, W2, lay_mid, 0)
    fine_step(off, span, SWEEPS)

    g2 = coarse_part(1, lambda p: u[1 + W1 + p])
    for copy in g2:
        copy.wait()
    kp[pad:pad + cx] = chain(1)

    def finish(q, _):
        f = kp[pad + bx * s + q]
        rows = jnp.concatenate([
            jnp.concatenate([u[1 + W1 + 4 * q + r, t * zs + c] + f for c in range(zs)], 1)
            for r in range(4) for t in range(ts)], 0)
        moved = permute(rows, from_tiles)
        for r in range(4):
            for t in range(ts):
                for c in range(zs):
                    at = (r * ts + t) * cy
                    raw[c, 4 * q + r, pl.ds(t, cy, stride=ts), :] = moved[at:at + cy, c * lanes:(c + 1) * lanes]
        return 0
    lax.fori_loop(0, bx, finish, 0)
    stores = [pltpu.make_async_copy(raw.at[c], out.at[0, :, :, pl.ds(c * lanes, lanes)], in_sem.at[c])
              for c in range(zs)]
    for store in stores:
        store.start()

    @pl.when(first_slice & has_lo)
    def _():
        ih_lo.wait_send()

    @pl.when(first_slice & has_hi)
    def _():
        ih_hi.wait_send()

    @pl.when(has_next)
    def _():
        f_own.wait_send()
        c_copy.wait_send()
        for stage in range(2):
            remote(es.at[stage], er.at[stage], e_ss.at[stage], e_rs.at[stage], (n + 1, s)).wait_send()

    @pl.when(has_next & has_lo)
    def _():
        f_lo.wait_send()

    @pl.when(has_next & has_hi)
    def _():
        f_hi.wait_send()

    for store in stores:
        store.wait()


def solution(mesh):
    n_count, s_count = mesh.shape["tm"], mesh.shape["space"]

    def on_device(init, labels, rates, heat):
        planes, ny, nz = init.shape
        bx, cy, cz = labels.shape
        cx = bx * s_count
        lanes = 128
        tile = (ny * nz // (cy * lanes), cy, lanes)
        pad = W1 // 4
        ext = planes + 2 * W1
        dma = pltpu.SemaphoreType.DMA

        def vm(*shape):
            return pltpu.VMEM(shape, F32)

        return pl.pallas_call(
            functools.partial(kernel, n_count, s_count),
            out_shape=jax.ShapeDtypeStruct((1, planes, ny, nz), F32),
            in_specs=[pl.BlockSpec(memory_space=pl.ANY)] * 4,
            out_specs=pl.BlockSpec(memory_space=pl.ANY),
            scratch_shapes=[
                vm(nz // lanes, planes, ny, lanes), pltpu.VMEM(labels.shape, labels.dtype),
                pltpu.SMEM((1, rates.shape[0]), F32), pltpu.SMEM(heat.shape, F32),
                dma((3 + nz // lanes,)), vm(planes, *tile),
                vm(2, cx + 2 * pad, cy, lanes),
                vm(2, cx, cy, lanes),
                vm(ext, *tile),
                vm(ext + 2, *tile),
                vm(ext, *tile), vm(ext // 4, cy, lanes), vm(ext // 4, cy, lanes), vm(ext // 4, cy, lanes),
                vm(planes, *tile),
                vm(planes + 2 * W2, *tile),
                vm(2, W2, *tile),
                vm(cx + 2 * pad, cy, lanes),
                vm(2, cx, cy, lanes), vm(2, cx, cy, lanes),
                vm(cx, cy, lanes), vm(cx, cy, lanes), vm(cx, cy, lanes),
                dma((3, s_count)), dma((3, s_count)),
                dma((2,)), dma((2,)),
                dma((3,)), dma((3,)),
                dma((2,)), dma((2,)),
                dma((2,)), dma((2,)),
                dma(()), dma(()),
            ],
            compiler_params=pltpu.CompilerParams(
                collective_id=0, has_side_effects=True, vmem_limit_bytes=48 * 1024 * 1024),
            name="parareal",
        )(init, labels, rates.reshape(1, -1), heat)

    return jax.shard_map(
        on_device,
        mesh=mesh,
        in_specs=(P("space", None, None), P("space", None, None), P(), P()),
        out_specs=P("tm", "space", None, None),
        check_vma=False,
    )
```

```python
import functools

import jax
import jax.numpy as jnp
from jax import lax
from jax.experimental import pallas as pl
from jax.experimental.pallas import tpu as pltpu
from jax.sharding import PartitionSpec as P

FINE_STEPS = 2
SWEEPS = 8
C_SWEEPS = 4
W1 = FINE_STEPS * SWEEPS
W2 = SWEEPS
F32 = jnp.float32
BF16 = jnp.bfloat16
MESH = pl.DeviceIdType.MESH
HI = lax.Precision.HIGHEST


def dot(a, b):
    return jnp.dot(a, b, precision=HI, preferred_element_type=F32)


def kernel(
    n_count, s_count,
    init_hbm, labels_hbm, rates_hbm, heat_hbm,
    out,
    raw, labels, rates, heat, in_sem, init,
    ag, gag, t0, u, sc, wt, inv, src, fs, fr, mid, kp, es, er, cs, cr, dcur,
    ag_ss, ag_rs, ih_ss, ih_rs, f_ss, f_rs, m_ss, m_rs, e_ss, e_rs, c_ss, c_rs,
):
    n = lax.axis_index("tm")
    s = lax.axis_index("space")
    planes, ny, nz = init_hbm.shape
    bx, cy, cz = labels_hbm.shape
    cx = bx * s_count
    lanes = ag.shape[-1]
    ts, zs = ny // cy, nz // lanes
    regions = rates_hbm.shape[1]
    pad = W1 // 4
    has_prev, has_next = n > 0, n < n_count - 1
    has_lo, has_hi = s > 0, s < s_count - 1

    pairs = [(labels_hbm, labels), (rates_hbm, rates), (heat_hbm, heat)]
    pairs += [(init_hbm.at[:, :, pl.ds(c * lanes, lanes)], raw.at[c]) for c in range(zs)]
    fetches = [pltpu.make_async_copy(a, b, in_sem.at[i]) for i, (a, b) in enumerate(pairs)]
    for fetch in fetches:
        fetch.start()

    barrier = pltpu.get_barrier_semaphore()
    def greet(cond, dev):
        @pl.when(cond)
        def _():
            pl.semaphore_signal(barrier, inc=1, device_id=dev, device_id_type=MESH)
    def one(c):
        return jnp.where(c, 1, 0).astype(jnp.int32)
    for j in range(1, s_count):
        pl.semaphore_signal(
            barrier, inc=1, device_id=(n, lax.rem(s + j, s_count)), device_id_type=MESH)
    partners = s_count - 1
    for cond_n, dn in ((has_prev, -1), (has_next, 1)):
        for cond_s, ds in ((None, 0), (has_lo, -1), (has_hi, 1)):
            cond = cond_n if cond_s is None else cond_n & cond_s
            greet(cond, (n + dn, s + ds))
            partners = partners + one(cond)
    pl.semaphore_wait(barrier, partners)

    def remote(a, b, ss, rs, dev):
        return pltpu.make_async_remote_copy(
            src_ref=a, dst_ref=b, send_sem=ss, recv_sem=rs, device_id=dev, device_id_type=MESH)

    half = 4 // zs

    def restrict(planes4):
        total = planes4[0]
        for extra in planes4[1:]:
            total = total + extra
        part = total[0]
        for k in range(1, ts * zs):
            part = part + total[k]
        lane = lax.broadcasted_iota(jnp.int32, part.shape, 1)
        step = 1
        while step < half:
            swap = jnp.where(lane % (2 * step) < step,
                             pltpu.roll(part, lanes - step, 1), pltpu.roll(part, step, 1))
            part = part + swap
            step *= 2
        return part * F32(1.0 / 64.0)

    def lookup(lab, row):
        total = jnp.zeros(lab.shape, F32)
        for r in range(regions):
            total = total + jnp.where(lab == F32(r), row(r), F32(0.0))
        return total

    crow = lax.broadcasted_iota(jnp.int32, (cx, cy, lanes), 1)
    ccol = lax.broadcasted_iota(jnp.int32, (cx, cy, lanes), 2)
    c_first, c_last = crow == 0, crow == cy - 1
    cz_first, cz_last = ccol < half, ccol >= lanes - half
    czero = jnp.zeros((1, cy, lanes), F32)

    def c_neighbours(w):
        total = jnp.concatenate([czero, w[:-1]], 0) + jnp.concatenate([w[1:], czero], 0)
        total = total + (jnp.where(c_first, F32(0.0), pltpu.roll(w, 1, 1))
                         + jnp.where(c_last, F32(0.0), pltpu.roll(w, cy - 1, 1)))
        return total + (jnp.where(cz_first, F32(0.0), pltpu.roll(w, half, 2))
                        + jnp.where(cz_last, F32(0.0), pltpu.roll(w, lanes - half, 2)))

    def c_jacobi(scaled, w, c_weight):
        for _ in range(C_SWEEPS):
            w = scaled + c_weight * c_neighbours(w)
        return w

    row = lax.broadcasted_iota(jnp.int32, (cy, lanes), 0)
    col = lax.broadcasted_iota(jnp.int32, (cy, lanes), 1)
    y_first, y_last = row == 0, row == cy - 1
    z_first, z_last = col == 0, col == lanes - 1

    def in_plane(w, k):
        t, c = k // zs, k % zs
        if t > 0:
            a = w[k - zs]
        else:
            a = jnp.where(y_first, F32(0.0), pltpu.roll(w[(ts - 1) * zs + c], 1, 0))
        if t < ts - 1:
            b = w[k + zs]
        else:
            b = jnp.where(y_last, F32(0.0), pltpu.roll(w[c], cy - 1, 0))
        if c > 0:
            d = w[k - 1]
        else:
            d = jnp.where(z_first, F32(0.0), pltpu.roll(w[k + zs - 1], 1, 1))
        if c < zs - 1:
            e = w[k + 1]
        else:
            e = jnp.where(z_last, F32(0.0), pltpu.roll(w[k - zs + 1], lanes - 1, 1))
        return (a + b) + (d + e)

    tiles = ts * zs

    def fine_step(first, length, shrink):
        def scale(q, _):
            g = first // 4 + q
            iv, so = inv[g], src[g]
            for r in range(4):
                p = first + 4 * q + r
                for k in range(tiles):
                    sc[p, k] = (u[p + 1, k] + so) * iv
            return 0
        lax.fori_loop(0, length // 4, scale, 0)

        def sweep(i, _):
            cut = 4 * (i // 4)
            lo = first + cut

            def quad(q, carry):
                before, cur = carry
                we = wt[lo // 4 + q]
                for r in range(4):
                    p = lo + 4 * q + r
                    after = [u[p + 2, k] for k in range(tiles)]
                    for k in range(tiles):
                        u[p + 1, k] = sc[p, k] + we * ((before[k] + after[k]) + in_plane(cur, k))
                    before, cur = cur, after
                return before, cur

            lax.fori_loop(0, (length - 2 * cut) // 4, quad,
                          ([u[lo, k] for k in range(tiles)], [u[lo + 1, k] for k in range(tiles)]))
            return 0
        lax.fori_loop(0, shrink, sweep, 0)

    def gather_start(stage, ref, mine):
        copies = []
        for j in range(1, s_count):
            copy = remote(mine(ref), mine(ref), ag_ss.at[stage, j], ag_rs.at[stage, j],
                          (n, lax.rem(s + j, s_count)))
            copy.start()
            copies.append(copy)
        return copies

    own = pl.ds(pad + bx * s, bx)

    ext = W1 * 2 + planes
    zero_block = jnp.zeros((pad, cy, lanes), F32)
    for k in (0, pad + cx):
        ag[0, k:k + pad] = zero_block
        ag[1, k:k + pad] = zero_block - 1.0
        kp[k:k + pad] = zero_block
    def zeros(*lead):
        return jnp.zeros(lead + (tiles, cy, lanes), F32)

    zero_fine = zeros()
    u[0] = zero_fine
    u[ext + 1] = zero_fine

    for fetch in fetches:
        fetch.wait()

    zi = lax.broadcasted_iota(jnp.int32, (nz, nz), 0)
    zj = lax.broadcasted_iota(jnp.int32, (nz, nz), 1)
    to_tiles = jnp.where(zi == zs * (zj % lanes) + zj // lanes, F32(1.0), F32(0.0)).astype(BF16)
    from_tiles = jnp.where(zj == zs * (zi % lanes) + zi // lanes, F32(1.0), F32(0.0)).astype(BF16)

    def permute(rows, one_hot):
        high = rows.astype(BF16)
        rest = rows - high.astype(F32)
        middle = rest.astype(BF16)
        low = (rest - middle.astype(F32)).astype(BF16)
        parts = [jnp.dot(x, one_hot, preferred_element_type=F32) for x in (high, middle, low)]
        return (parts[0] + parts[1]) + parts[2]

    def load(q, _):
        rows = jnp.concatenate([
            jnp.concatenate([raw[c, 4 * q + r, pl.ds(t, cy, stride=ts), :] for c in range(zs)], 1)
            for r in range(4) for t in range(ts)], 0)
        moved = permute(rows, to_tiles)
        for r in range(4):
            for t in range(ts):
                for c in range(zs):
                    at = (r * ts + t) * cy
                    init[4 * q + r, t * zs + c] = moved[at:at + cy, c * lanes:(c + 1) * lanes]
        return 0
    lax.fori_loop(0, bx, load, 0)

    li = lax.broadcasted_iota(jnp.int32, (cz, lanes), 0)
    lj = lax.broadcasted_iota(jnp.int32, (cz, lanes), 1)
    spread = jnp.where(li == lj // half, F32(1.0), F32(0.0))
    for k in range(bx):
        ag[0, pad + bx * s + k] = restrict([init[4 * k + r] for r in range(4)])
        ag[1, pad + bx * s + k] = dot(labels[k].astype(F32), spread)
    g0 = gather_start(0, ag, lambda r: r.at[:, own])

    first_slice = n == 0
    ih_lo = remote(init, t0.at[pl.ds(W1 + planes, W1)], ih_ss.at[0], ih_rs.at[0], (n, s - 1))
    ih_hi = remote(init, t0.at[pl.ds(0, W1)], ih_ss.at[1], ih_rs.at[1], (n, s + 1))

    @pl.when(first_slice & has_lo)
    def _():
        ih_lo.start()

    @pl.when(first_slice & has_hi)
    def _():
        ih_hi.start()

    @pl.when(jnp.logical_not(has_lo))
    def _():
        t0[0:W1] = zeros(W1)
        fr[0:W2] = zeros(W2)
        mid[0] = zeros(W2)

    @pl.when(jnp.logical_not(has_hi))
    def _():
        t0[W1 + planes:] = zeros(W1)
        fr[W2 + planes:] = zeros(W2)
        mid[1] = zeros(W2)

    for copy in g0:
        copy.wait()

    lab = ag[1, pl.ds(bx * s, ext // 4)]
    rate = lookup(lab, lambda r: rates[0, r])
    iv = 1.0 / (1.0 + 6.0 * rate)
    inv[...] = iv
    wt[...] = rate * iv
    src[...] = lookup(lab, lambda r: heat[n, r])

    lab_all = ag[1, pad:pad + cx]
    c_rate = FINE_STEPS * lookup(lab_all, lambda r: rates[0, r]) / 16.0
    c_inv = 1.0 / (1.0 + 6.0 * c_rate)
    c_weight = c_rate * c_inv

    def advance(m, c):
        source = FINE_STEPS * lookup(lab_all, lambda r: heat[m, r])
        return c_jacobi((c + source) * c_inv, c, c_weight)

    own_c = lax.fori_loop(0, n, advance, ag[0, pad:pad + cx])
    dcur[...] = advance(n, own_c)
    kp[pad:pad + cx] = own_c

    @pl.when(first_slice)
    def _():
        @pl.when(has_hi)
        def _():
            ih_lo_wait = remote(init, t0.at[pl.ds(W1 + planes, W1)], ih_ss.at[0], ih_rs.at[0], (n, s + 1))
            ih_lo_wait.wait_recv()

        @pl.when(has_lo)
        def _():
            ih_hi_wait = remote(init, t0.at[pl.ds(0, W1)], ih_ss.at[1], ih_rs.at[1], (n, s - 1))
            ih_hi_wait.wait_recv()

        def lay(p, _):
            u[1 + p] = t0[p]
            u[1 + W1 + planes + p] = t0[W1 + planes + p]
            return 0
        lax.fori_loop(0, W1, lay, 0)

        def lay_own(p, _):
            u[1 + W1 + p] = init[p]
            return 0
        lax.fori_loop(0, planes, lay_own, 0)

    @pl.when(has_prev)
    def _():
        def lay(k, _):
            f = kp[bx * s + k]
            for r in range(4):
                for q in range(tiles):
                    u[1 + 4 * k + r, q] = f
            return 0
        lax.fori_loop(0, ext // 4, lay, 0)

    fine_step(0, ext, SWEEPS)
    fine_step(SWEEPS, ext - 2 * SWEEPS, SWEEPS)

    own_g = pl.ds(bx * s, bx)

    def coarse_part(stage, plane_of):
        for k in range(bx):
            gag[stage, bx * s + k] = restrict([plane_of(4 * k + r) for r in range(4)])
        copies = gather_start(stage + 1, gag.at[stage], lambda r: r.at[own_g])
        return copies

    def keep(p, _):
        fs[p] = u[1 + W1 + p]
        return 0
    lax.fori_loop(0, planes, keep, 0)
    g1 = coarse_part(0, lambda p: fs[p])

    f_own = remote(fs, fr.at[pl.ds(W2, planes)], f_ss.at[0], f_rs.at[0], (n + 1, s))
    f_lo = remote(fs.at[pl.ds(0, W2)], fr.at[pl.ds(W2 + planes, W2)], f_ss.at[1], f_rs.at[1], (n + 1, s - 1))
    f_hi = remote(fs.at[pl.ds(planes - W2, W2)], fr.at[pl.ds(0, W2)], f_ss.at[2], f_rs.at[2], (n + 1, s + 1))

    @pl.when(has_next)
    def _():
        f_own.start()

    @pl.when(has_next & has_lo)
    def _():
        f_lo.start()

    @pl.when(has_next & has_hi)
    def _():
        f_hi.start()

    for copy in g1:
        copy.wait()

    def chain(stage):
        e_copy = remote(es.at[stage], er.at[stage], e_ss.at[stage], e_rs.at[stage], (n + 1, s))

        @pl.when(first_slice)
        def _():
            er[stage] = jnp.zeros((cx, cy, lanes), F32)

        @pl.when(has_prev)
        def _():
            e_copy.wait_recv()
        e = er[stage]
        corr = c_jacobi(e * c_inv, e, c_weight)
        rf = gag[stage]
        es[stage] = corr + (rf - dcur[...])

        @pl.when(has_next)
        def _():
            e_copy.start()
        dcur[...] = rf + corr
        return corr

    cs[...] = chain(0)
    c_copy = remote(cs, cr, c_ss, c_rs, (n + 1, s))

    @pl.when(has_next)
    def _():
        c_copy.start()

    off = W1 - W2
    span = planes + 2 * W2

    @pl.when(has_prev)
    def _():
        c_copy.wait_recv()
        f_own.wait_recv()

        @pl.when(has_hi)
        def _():
            f_lo.wait_recv()

        @pl.when(has_lo)
        def _():
            f_hi.wait_recv()
        kp[pad:pad + cx] = cr[...]

        def lay(k, _):
            f = kp[bx * s + off // 4 + k]
            for r in range(4):
                for q in range(tiles):
                    u[1 + off + 4 * k + r, q] = fr[4 * k + r, q] + f
            return 0
        lax.fori_loop(0, span // 4, lay, 0)

    @pl.when(has_prev)
    def _():
        fine_step(off, span, SWEEPS)

        m_lo = remote(u.at[pl.ds(1 + W1, W2)], mid.at[1], m_ss.at[0], m_rs.at[0], (n, s - 1))
        m_hi = remote(u.at[pl.ds(1 + W1 + planes - W2, W2)], mid.at[0], m_ss.at[1], m_rs.at[1], (n, s + 1))

        @pl.when(has_lo)
        def _():
            m_lo.start()

        @pl.when(has_hi)
        def _():
            m_hi.start()

        @pl.when(has_lo)
        def _():
            m_hi.wait_recv()
            m_lo.wait_send()

        @pl.when(has_hi)
        def _():
            m_lo.wait_recv()
            m_hi.wait_send()

        def lay_mid(p, _):
            u[1 + off + p] = mid[0, p]
            u[1 + W1 + planes + p] = mid[1, p]
            return 0
        lax.fori_loop(0, W2, lay_mid, 0)
        fine_step(off, span, SWEEPS)

    g2 = coarse_part(1, lambda p: u[1 + W1 + p])
    for copy in g2:
        copy.wait()
    kp[pad:pad + cx] = chain(1)

    def finish(q, _):
        f = kp[pad + bx * s + q]
        rows = jnp.concatenate([
            jnp.concatenate([u[1 + W1 + 4 * q + r, t * zs + c] + f for c in range(zs)], 1)
            for r in range(4) for t in range(ts)], 0)
        moved = permute(rows, from_tiles)
        for r in range(4):
            for t in range(ts):
                for c in range(zs):
                    at = (r * ts + t) * cy
                    raw[c, 4 * q + r, pl.ds(t, cy, stride=ts), :] = moved[at:at + cy, c * lanes:(c + 1) * lanes]
        return 0
    lax.fori_loop(0, bx, finish, 0)
    stores = [pltpu.make_async_copy(raw.at[c], out.at[0, :, :, pl.ds(c * lanes, lanes)], in_sem.at[c])
              for c in range(zs)]
    for store in stores:
        store.start()

    @pl.when(first_slice & has_lo)
    def _():
        ih_lo.wait_send()

    @pl.when(first_slice & has_hi)
    def _():
        ih_hi.wait_send()

    @pl.when(has_next)
    def _():
        f_own.wait_send()
        c_copy.wait_send()
        for stage in range(2):
            remote(es.at[stage], er.at[stage], e_ss.at[stage], e_rs.at[stage], (n + 1, s)).wait_send()

    @pl.when(has_next & has_lo)
    def _():
        f_lo.wait_send()

    @pl.when(has_next & has_hi)
    def _():
        f_hi.wait_send()

    for store in stores:
        store.wait()


def solution(mesh):
    n_count, s_count = mesh.shape["tm"], mesh.shape["space"]

    def on_device(init, labels, rates, heat):
        planes, ny, nz = init.shape
        bx, cy, cz = labels.shape
        cx = bx * s_count
        lanes = 128
        tile = (ny * nz // (cy * lanes), cy, lanes)
        pad = W1 // 4
        ext = planes + 2 * W1
        dma = pltpu.SemaphoreType.DMA

        def vm(*shape):
            return pltpu.VMEM(shape, F32)

        return pl.pallas_call(
            functools.partial(kernel, n_count, s_count),
            out_shape=jax.ShapeDtypeStruct((1, planes, ny, nz), F32),
            in_specs=[pl.BlockSpec(memory_space=pl.ANY)] * 4,
            out_specs=pl.BlockSpec(memory_space=pl.ANY),
            scratch_shapes=[
                vm(nz // lanes, planes, ny, lanes), pltpu.VMEM(labels.shape, labels.dtype),
                pltpu.SMEM((1, rates.shape[0]), F32), pltpu.SMEM(heat.shape, F32),
                dma((3 + nz // lanes,)), vm(planes, *tile),
                vm(2, cx + 2 * pad, cy, lanes),
                vm(2, cx, cy, lanes),
                vm(ext, *tile),
                vm(ext + 2, *tile),
                vm(ext, *tile), vm(ext // 4, cy, lanes), vm(ext // 4, cy, lanes), vm(ext // 4, cy, lanes),
                vm(planes, *tile),
                vm(planes + 2 * W2, *tile),
                vm(2, W2, *tile),
                vm(cx + 2 * pad, cy, lanes),
                vm(2, cx, cy, lanes), vm(2, cx, cy, lanes),
                vm(cx, cy, lanes), vm(cx, cy, lanes), vm(cx, cy, lanes),
                dma((3, s_count)), dma((3, s_count)),
                dma((2,)), dma((2,)),
                dma((3,)), dma((3,)),
                dma((2,)), dma((2,)),
                dma((2,)), dma((2,)),
                dma(()), dma(()),
            ],
            compiler_params=pltpu.CompilerParams(
                collective_id=0, has_side_effects=True, vmem_limit_bytes=48 * 1024 * 1024),
            name="parareal",
        )(init, labels, rates.reshape(1, -1), heat)

    return jax.shard_map(
        on_device,
        mesh=mesh,
        in_specs=(P("space", None, None), P("space", None, None), P(), P()),
        out_specs=P("tm", "space", None, None),
        check_vma=False,
    )
```
